256 devices in a mesh: dp: 32 (over x, z_hi, core), tensor: 8 (over y, z_lo).
Axes of the slice: x: 4, y: 4, z: 8 (z_hi: 4, z_lo: 2; z = z_hi * 2 + z_lo), core: 2. Of those that a mesh axis runs over, the one named last changes fastest.
Arguments:
- tokens: bfloat16 [32, 256, 8192], P('dp', None, 'tensor'), may hold values from -6 to 6
- segment_ids: int32 [32, 256], P('dp'), may hold values from 0 to 3, never falling along the last dimension, each value on 1 to 128 neighbouring positions
- queries: bfloat16 [32, 256, 8192], P('dp', None, 'tensor'), may hold values from -7 to 7
- teacher_keys: bfloat16 [32, 256, 1024], P('dp', None, 'tensor'), may hold values from -7 to 7
- teacher_values: bfloat16 [32, 256, 1024], P('dp', None, 'tensor'), may hold values from -6 to 6
- down_weight: bfloat16 [8192, 512], P('tensor'), may hold values from -0.0625 to 0.0625
- rope_weight: bfloat16 [64, 8192], P(None, 'tensor'), may hold values from -1 to 1
- key_up: bfloat16 [512, 4096], P(None, 'tensor'), may hold values from -0.25 to 0.25
- value_up: bfloat16 [512, 8192], P(None, 'tensor'), may hold values from -0.25 to 0.25
Outputs:
- grad_down: float32 [8192, 512], P('tensor')
- grad_rope: float32 [64, 8192], P(None, 'tensor')
- grad_key_up: float32 [512, 4096], P(None, 'tensor')
- grad_value_up: float32 [512, 8192], P(None, 'tensor')
The draws below stay inside these ranges and needn't reach their ends.
Inputs may be any that keep to these rules, and one draw needn't show every extreme that they name: `segment_ids`: along a sequence the document number never falls; each of the 4 documents holds 1 to 128 tokens, and one holds exactly 128.
All inputs are finite; a program needn't handle non-finite values.
Results may differ from the reference program's by a relative error of at most 0.011.
Values sent between devices are 32-bit elements; how exact they have to be, the bound alone decides.
No kernel may reach another device: no remote copies, remote signals or barrier semaphores. Data moves between devices by JAX's collectives and lax.ppermute only.
A program may use at most 64 MiB of HBM per device.

```python
import math
import jax
import jax.numpy as jnp
import numpy as np
from jax import lax

D = 8192
HEADS = 64
KVH = 8
HEAD = 128
LATENT = 512
ROPE = 64
SEQ = 256
DOCS = 4
SEQS = 32


plant_strengths = (4.0, 5.5, 7.0)


key_size = 7.0


token_size = 4.0


rope_pull = 3.0


def entry_masks():
    entry_index = jnp.arange(HEAD, dtype=jnp.int32)
    teacher_low = entry_index % (HEAD // 2) >= HEAD // 8
    rope_low = entry_index % (ROPE // 2) >= ROPE // 8
    in_rope = entry_index < ROPE
    planted = teacher_low & jnp.where(in_rope, rope_low, True)
    return (planted, planted & in_rope)


def sign_pattern(key):
    coin_flips = jax.random.randint(jax.random.fold_in(key, 101), (HEAD,), 0, 2)
    return (2 * coin_flips - 1).astype(jnp.float32)


def token_direction(key):
    coin_flips = jax.random.randint(jax.random.fold_in(key, 102), (D,), 0, 2)
    return (2 * coin_flips - 1).astype(jnp.float32)


def plant_positions(key):
    quarter = SEQ // 4
    offsets = jax.random.randint(jax.random.fold_in(key, 103), (SEQS, 3), 0, quarter - 3)
    return jnp.arange(3, dtype=jnp.int32)[None, :] * quarter + 2 + offsets


def row_hits(key, shift):
    plant_rows = plant_positions(key) - shift
    position = jnp.arange(SEQ, dtype=jnp.int32)
    return (position[None, :, None] == plant_rows[:, None, :]).astype(jnp.float32)


def clipped_normal(key, array_shape):
    return jnp.clip(jax.random.normal(key, array_shape, jnp.float32), -6.0, 6.0)


def draw_queries(key, part):
    planted, rope_planted = entry_masks()
    sign_row = sign_pattern(key)
    strengths = jnp.array(plant_strengths, jnp.float32)
    main_hits = row_hits(key, 0)
    row_strength = jnp.sum(main_hits * strengths[None, None, :], axis=-1)
    row_planted = jnp.sum(main_hits, axis=-1) > 0.5
    entry_scale = jnp.where(rope_planted, 1.0, jnp.where(planted, 2.0 / 3.0, 0.0)) * sign_row
    noise_part = clipped_normal(jax.random.fold_in(key, 1), (SEQS, SEQ, HEADS, HEAD))
    plant_value = jnp.where(planted[None, None, None, :], row_strength[:, :, None, None] * entry_scale[None, None, None, :], 0.1 * noise_part)
    values = jnp.where(row_planted[:, :, None, None], plant_value, noise_part)
    return values.reshape(SEQS, SEQ, HEADS * HEAD).astype(jnp.bfloat16)


def draw_teacher_keys(key, part):
    planted, unused_mask = entry_masks()
    sign_row = sign_pattern(key)
    main_planted = jnp.sum(row_hits(key, 0), axis=-1) > 0.5
    prev_planted = jnp.sum(row_hits(key, 1), axis=-1) > 0.5
    entry_index = jnp.arange(HEAD, dtype=jnp.int32)
    prev_entries = planted & (entry_index < HEAD - 1)
    noise_part = clipped_normal(jax.random.fold_in(key, 2), (SEQS, SEQ, KVH, HEAD))
    main_value = jnp.where(planted[None, None, None, :], key_size * sign_row[None, None, None, :], 0.1 * noise_part)
    prev_value = jnp.where(prev_entries[None, None, None, :], key_size * sign_row[None, None, None, :], 0.1 * noise_part)
    values = jnp.where(main_planted[:, :, None, None], main_value, jnp.where(prev_planted[:, :, None, None], prev_value, noise_part))
    return values.reshape(SEQS, SEQ, KVH * HEAD).astype(jnp.bfloat16)


def draw_tokens(key, part):
    unused_mask, rope_planted = entry_masks()
    rope_count = jnp.sum(rope_planted.astype(jnp.float32))
    strengths = jnp.array(plant_strengths, jnp.float32)
    row_gain = strengths * rope_pull * rope_count / math.sqrt(HEAD)
    prev_size = token_size - 2.0 / row_gain
    main_hits = row_hits(key, 0)
    prev_hits = row_hits(key, 1)
    row_scale = jnp.sum(main_hits * token_size + prev_hits * prev_size[None, None, :], axis=-1)
    row_planted = jnp.sum(main_hits + prev_hits, axis=-1) > 0.5
    direction = token_direction(key)
    noise_part = clipped_normal(jax.random.fold_in(key, 3), (SEQS, SEQ, D))
    values = jnp.where(row_planted[:, :, None], row_scale[:, :, None] * direction[None, None, :] + 0.15 * noise_part, noise_part)
    return values.astype(jnp.bfloat16)


def draw_rope_weight(key, part):
    unused_mask, rope_planted = entry_masks()
    sign_row = sign_pattern(key)
    pull_rows = jnp.where(rope_planted[:ROPE], rope_pull, 0.0) * sign_row[:ROPE]
    direction = token_direction(key)
    noise_part = clipped_normal(jax.random.fold_in(key, 4), (ROPE, D)) / math.sqrt(D)
    return (noise_part + pull_rows[:, None] * direction[None, :] / D).astype(jnp.bfloat16)


def shard_levels(own_key, shape, pieces, smallest, high):
    loudness, own = 1.0, jax.random.fold_in(own_key, 6)
    for dim, parts in pieces:
        heights = jnp.exp(jax.random.uniform(jax.random.fold_in(own, dim), (parts,), jnp.float32, smallest / len(pieces), high / len(pieces)))
        loudness = loudness * jnp.repeat(heights, shape[dim] // parts).reshape([-1 if axis == dim else 1 for axis in range(len(shape))])
    return loudness


def split_up(amount, total, most, slope):
    loads = [(1 << 20) // math.isqrt(rank ** slope) + 1 for rank in range(2, amount + 1)]
    spare, counts = total - most - (amount - 1), [1] * (amount - 1)
    while spare > 0:
        free = [i for i in range(amount - 1) if counts[i] < most]
        whole, remaining = sum([loads[i] for i in free]), spare
        for i in free:
            more = min(most - counts[i], max(1, remaining * loads[i] // whole), spare)
            counts[i] = counts[i] + more
            spare = spare - more
    return np.array([most] + counts)


def ragged(key, amount, total, bound, slope):
    if amount == 2:
        one = jax.random.randint(key, (), max(1, total - bound), min(bound, total - 1) + 1)
        return jnp.stack([one, total - one])
    sizes = jnp.asarray(split_up(amount, total, bound, slope), jnp.int32)
    couples = (amount - 1) // 2
    source_of, receiver = sizes[1:1 + 2 * couples:2], sizes[2:2 + 2 * couples:2]
    slack = jnp.minimum(source_of - 1, bound - receiver)
    passed = jax.random.randint(jax.random.fold_in(key, 1), (couples,), 0, 1 << 20) % (slack + 1)
    sizes = sizes.at[1:1 + 2 * couples:2].set(source_of - passed).at[2:2 + 2 * couples:2].set(receiver + passed)
    return sizes[jax.random.permutation(jax.random.fold_in(key, 2), amount)]


def gaussian(stream_key, dims, scale, limit, pieces=(), held_as=jnp.bfloat16):
    result = jax.random.normal(stream_key, dims, jnp.float32) * scale
    if len(pieces) > 0:
        result = shard_levels(stream_key, dims, pieces, -0.22, 0.18) * result
    return jnp.clip(result, min=-limit, max=limit).astype(held_as)


def setup_inputs(seed: int = 0) -> dict:
    splits = jax.random.split(jax.random.key(seed), 10)
    tokens = draw_tokens(jax.random.fold_in(splits[9], 71), 0)
    segment_ids = jax.vmap(lambda own: jnp.searchsorted(jnp.cumsum(ragged(own, DOCS, SEQ, SEQ // 2, 2)), jnp.arange(SEQ), side="right"))(jax.random.split(splits[1], SEQS)).reshape((SEQS, SEQ)).astype(jnp.int32)
    queries = draw_queries(jax.random.fold_in(splits[9], 71), 0)
    teacher_keys = draw_teacher_keys(jax.random.fold_in(splits[9], 71), 0)
    teacher_values = gaussian(splits[4], (SEQS, SEQ, KVH * HEAD), 1.0, 6.0, ((0, 32), (2, 8)))
    down_weight = gaussian(splits[5], (D, LATENT), D ** -0.5, 0.0625, ((0, 8),))
    rope_weight = draw_rope_weight(jax.random.fold_in(splits[9], 71), 0)
    key_up = gaussian(splits[7], (LATENT, HEADS * (HEAD - ROPE)), LATENT ** -0.5, 0.25, ((1, 8),))
    value_up = gaussian(splits[8], (LATENT, HEADS * HEAD), LATENT ** -0.5, 0.25, ((1, 8),))
    return dict(tokens=tokens, segment_ids=segment_ids, queries=queries, teacher_keys=teacher_keys, teacher_values=teacher_values, down_weight=down_weight, rope_weight=rope_weight, key_up=key_up, value_up=value_up)


theta_base = 500000.0
norm_eps = 1e-06

def angle_tables(positions, width):
    half_width = width // 2
    exponent = jnp.arange(half_width, dtype=jnp.float32) * (2.0 / width)
    frequency = jnp.exp(-exponent * jnp.log(jnp.float32(theta_base)))
    angles = positions.astype(jnp.float32)[:, None] * frequency[None, :]
    return (jnp.cos(angles), jnp.sin(angles))

def rotate_last(tensor, cosine, sine_tab):
    half_width = tensor.shape[-1] // 2
    first_half = tensor[..., :half_width]
    second_half = tensor[..., half_width:]
    return jnp.concatenate([first_half * cosine - second_half * sine_tab, second_half * cosine + first_half * sine_tab], axis=-1)

def rotate_rows(matrix, cosine, sine_tab):
    half_width = matrix.shape[0] // 2
    first_half = matrix[:half_width]
    second_half = matrix[half_width:]
    return jnp.concatenate([first_half * cosine - second_half * sine_tab, second_half * cosine + first_half * sine_tab], axis=0)

def unrotate_rows(matrix, cosine, sine_tab):
    half_width = matrix.shape[0] // 2
    first_half = matrix[:half_width]
    second_half = matrix[half_width:]
    return jnp.concatenate([first_half * cosine + second_half * sine_tab, second_half * cosine - first_half * sine_tab], axis=0)

def doc_positions(segments_row):
    position_index = jnp.arange(segments_row.shape[0], dtype=jnp.int32)
    is_start = jnp.concatenate([jnp.ones((1,), dtype=jnp.bool_), segments_row[1:] != segments_row[:-1]])
    doc_start = lax.cummax(jnp.where(is_start, position_index, 0).astype(jnp.int32), axis=0)
    return position_index - doc_start

def masked_softmax(scores, doc_mask):
    masked = jnp.where(doc_mask > 0, scores, -jnp.inf)
    peak = lax.optimization_barrier(jnp.max(masked, axis=-1, keepdims=True))
    weights = jnp.exp(masked - peak)
    return weights / lax.optimization_barrier(jnp.sum(weights, axis=-1, keepdims=True))

def sequence_grads(token_rows, segments_row, queries_row, tkeys_row, tvalues_row, down_weight, rope_weight, key_up, value_up):
    seq_len = token_rows.shape[0]
    nope_width = HEAD - ROPE
    group_size = HEADS // KVH
    score_scale = 1.0 / math.sqrt(HEAD)
    f32 = jnp.float32
    bf16 = jnp.bfloat16
    positions = doc_positions(segments_row)
    position_index = jnp.arange(seq_len, dtype=jnp.int32)
    doc_mask = ((segments_row[:, None] == segments_row[None, :]) & (position_index[None, :] <= position_index[:, None])).astype(jnp.int32)
    cos_full, sin_full = angle_tables(positions, HEAD)
    cos_rope, sin_rope = angle_tables(positions, ROPE)
    latent_raw = jnp.dot(token_rows, down_weight, preferred_element_type=f32)
    inv_rms = lax.rsqrt(lax.optimization_barrier(jnp.mean(latent_raw * latent_raw, axis=-1, keepdims=True)) + norm_eps)
    normed = latent_raw * inv_rms
    latent = normed.astype(bf16)
    rope_raw = lax.dot_general(rope_weight, token_rows, (((1,), (1,)), ((), ())), preferred_element_type=f32)
    rope_key = rotate_rows(rope_raw, cos_rope.T, sin_rope.T).astype(bf16)
    head_queries = queries_row.reshape(seq_len, HEADS, HEAD).transpose(1, 0, 2)
    teacher_q = rotate_last(head_queries.astype(f32), cos_full, sin_full).astype(bf16).reshape(KVH, group_size, seq_len, HEAD)
    teacher_k = rotate_last(tkeys_row.reshape(seq_len, KVH, HEAD).transpose(1, 0, 2).astype(f32), cos_full, sin_full).astype(bf16)
    teacher_v = tvalues_row.reshape(seq_len, KVH, HEAD).transpose(1, 0, 2)
    teacher_scores = jnp.einsum('kgqd,kpd->kgqp', teacher_q.astype(f32), teacher_k.astype(f32)) * score_scale
    teacher_weights = masked_softmax(teacher_scores, doc_mask).astype(bf16)
    teacher_out = jnp.einsum('kgqp,kpd->kgqd', teacher_weights.astype(f32), teacher_v.astype(f32)).reshape(HEADS, seq_len, HEAD)
    key_nope = jnp.dot(latent, key_up, preferred_element_type=f32).astype(bf16).reshape(seq_len, HEADS, nope_width).transpose(1, 0, 2)
    head_values = jnp.dot(latent, value_up, preferred_element_type=f32).astype(bf16).reshape(seq_len, HEADS, HEAD).transpose(1, 0, 2)
    rotated_q = rotate_last(head_queries[..., :ROPE].astype(f32), cos_rope, sin_rope).astype(bf16)
    student_q = jnp.concatenate([head_queries[..., ROPE:], rotated_q], axis=-1)
    student_k = jnp.concatenate([key_nope, jnp.broadcast_to(rope_key.T[None], (HEADS, seq_len, ROPE))], axis=-1)
    student_scores = jnp.einsum('hqd,hpd->hqp', student_q.astype(f32), student_k.astype(f32)) * score_scale
    student_weights = masked_softmax(student_scores, doc_mask)
    student_low = student_weights.astype(bf16)
    student_out = jnp.einsum('hqp,hpd->hqd', student_low.astype(f32), head_values.astype(f32))
    out_grad = (student_out - teacher_out).astype(bf16)
    weight_grad = jnp.einsum('hqd,hpd->hqp', out_grad.astype(f32), head_values.astype(f32))
    row_dot = lax.optimization_barrier(jnp.sum(student_weights * weight_grad, axis=-1, keepdims=True))
    score_grad = (student_weights * (weight_grad - row_dot) * score_scale).astype(bf16)
    value_grad = jnp.einsum('hqp,hqd->hpd', student_low.astype(f32), out_grad.astype(f32)).astype(bf16)
    key_grad = jnp.einsum('hqp,hqd->hpd', score_grad.astype(f32), student_q.astype(f32))
    nope_grad = key_grad[..., :nope_width].astype(bf16).transpose(1, 0, 2).reshape(seq_len, HEADS * nope_width)
    rope_sum = lax.optimization_barrier(jnp.sum(key_grad[..., nope_width:], axis=0)).T
    rope_grad = unrotate_rows(rope_sum, cos_rope.T, sin_rope.T).astype(bf16)
    value_flat = value_grad.transpose(1, 0, 2).reshape(seq_len, HEADS * HEAD)
    contract_cols = (((1,), (1,)), ((), ()))
    contract_rows = (((0,), (0,)), ((), ()))
    norm_grad = lax.dot_general(nope_grad, key_up, contract_cols, preferred_element_type=f32) + lax.dot_general(value_flat, value_up, contract_cols, preferred_element_type=f32)
    latent_grad = ((norm_grad - normed * lax.optimization_barrier(jnp.mean(norm_grad * normed, axis=-1, keepdims=True))) * inv_rms).astype(bf16)
    grad_down = lax.dot_general(token_rows, latent_grad, contract_rows, preferred_element_type=f32)
    grad_rope = jnp.dot(rope_grad, token_rows, preferred_element_type=f32)
    grad_kup = lax.dot_general(latent, nope_grad, contract_rows, preferred_element_type=f32)
    grad_vup = lax.dot_general(latent, value_flat, contract_rows, preferred_element_type=f32)
    return (grad_down, grad_rope, grad_kup, grad_vup)

def reference(tokens, segment_ids, queries, teacher_keys, teacher_values, down_weight, rope_weight, key_up, value_up):

    def accumulate(running, row_inputs):
        token_rows, segments_row, queries_row, tkeys_row, tvalues_row = row_inputs
        new_grads = sequence_grads(token_rows, segments_row, queries_row, tkeys_row, tvalues_row, down_weight, rope_weight, key_up, value_up)
        return (tuple((old_sum + new_grad for old_sum, new_grad in zip(running, new_grads))), None)
    zeros_init = (jnp.zeros(down_weight.shape, jnp.float32), jnp.zeros(rope_weight.shape, jnp.float32), jnp.zeros(key_up.shape, jnp.float32), jnp.zeros(value_up.shape, jnp.float32))
    totals, unused = lax.scan(accumulate, zeros_init, (tokens, segment_ids, queries, teacher_keys, teacher_values))
    return (totals[0], totals[1], totals[2], totals[3])
```

```python
import math

import jax
import jax.numpy as jnp
from jax import lax
from jax.sharding import PartitionSpec as P

HEAD = 128
ROPE = 64


theta_base = 500000.0
norm_eps = 1e-06


def angle_tables(positions, width):
    half_width = width // 2
    exponent = jnp.arange(half_width, dtype=jnp.float32) * (2.0 / width)
    frequency = jnp.exp(-exponent * jnp.log(jnp.float32(theta_base)))
    angles = positions.astype(jnp.float32)[:, None] * frequency[None, :]
    return (jnp.cos(angles), jnp.sin(angles))


def rotate_last(tensor, cosine, sine_tab):
    half_width = tensor.shape[-1] // 2
    first_half = tensor[..., :half_width]
    second_half = tensor[..., half_width:]
    return jnp.concatenate(
        [
            first_half * cosine - second_half * sine_tab,
            second_half * cosine + first_half * sine_tab,
        ],
        axis=-1,
    )


def rotate_rows(matrix, cosine, sine_tab):
    half_width = matrix.shape[0] // 2
    first_half = matrix[:half_width]
    second_half = matrix[half_width:]
    return jnp.concatenate(
        [
            first_half * cosine - second_half * sine_tab,
            second_half * cosine + first_half * sine_tab,
        ],
        axis=0,
    )


def unrotate_rows(matrix, cosine, sine_tab):
    half_width = matrix.shape[0] // 2
    first_half = matrix[:half_width]
    second_half = matrix[half_width:]
    return jnp.concatenate(
        [
            first_half * cosine + second_half * sine_tab,
            second_half * cosine - first_half * sine_tab,
        ],
        axis=0,
    )


def doc_positions(segments_row):
    position_index = jnp.arange(segments_row.shape[0], dtype=jnp.int32)
    is_start = jnp.concatenate(
        [jnp.ones((1,), dtype=jnp.bool_), segments_row[1:] != segments_row[:-1]]
    )
    doc_start = lax.cummax(jnp.where(is_start, position_index, 0), axis=0)
    return position_index - doc_start


def block_mask(seg_block, segments_row, row_start):
    rows_index = row_start + jnp.arange(seg_block.shape[0], dtype=jnp.int32)
    cols_index = jnp.arange(segments_row.shape[0], dtype=jnp.int32)
    return (
        (seg_block[:, None] == segments_row[None, :]) & (cols_index[None, :] <= rows_index[:, None])
    ).astype(jnp.int32)


def masked_softmax(scores, doc_mask):
    masked = jnp.where(doc_mask > 0, scores, -jnp.inf)
    peak = jnp.max(masked, axis=-1, keepdims=True)
    weights = jnp.exp(masked - peak)
    return weights / jnp.sum(weights, axis=-1, keepdims=True)

AXES = ("dp", "tensor")


def coords():
    d, t = lax.axis_index("dp"), lax.axis_index("tensor")
    return dict(x=d // 8, h=(d // 2) % 4, c=d % 2, y=t // 2, l=t % 2)


def permute(value, move):
    pairs = []
    for i in range(256):
        d, t = divmod(i, 8)
        at = dict(x=d // 8, h=(d // 2) % 4, c=d % 2, y=t // 2, l=t % 2)
        to = {**at, **move(at)}
        j = (to["x"] * 8 + to["h"] * 2 + to["c"]) * 8 + to["y"] * 2 + to["l"]
        pairs.append((i, j))
    return lax.ppermute(value, AXES, pairs)


def pick(value, index):
    return lax.dynamic_index_in_dim(value, index, 0, keepdims=False)


def flip(axis, mask):
    return lambda at: {axis: at[axis] ^ mask}


def ring_bits(i):
    return (i ^ (i >> 1)) & 1, (i >> 1) & 1


def scatter_ring(first, second, axis, i):
    f, g = ring_bits(i)
    first = first.reshape((2, 2) + first.shape[1:])
    second = second.reshape((2, 2) + second.shape[1:])
    got1 = permute(pick(first, 1 - f), flip(axis, 1))
    got2 = permute(pick(second, 1 - g), flip(axis, 3))
    first = pick(first, f) + got1
    second = pick(second, g) + got2
    got1 = permute(pick(first, 1 - g), flip(axis, 3))
    got2 = permute(pick(second, 1 - f), flip(axis, 1))
    return pick(first, g) + got1, pick(second, f) + got2


def join(own, other, i):
    return jnp.where(i == 0, jnp.stack([own, other]), jnp.stack([other, own]))


def gather_ring(first, second, axis, i):
    f, g = ring_bits(i)
    got1 = permute(first, flip(axis, 3))
    got2 = permute(second, flip(axis, 1))
    first, second = join(first, got1, g), join(second, got2, f)
    got1 = permute(first, flip(axis, 1))
    got2 = permute(second, flip(axis, 3))
    first, second = join(first, got1, f), join(second, got2, g)
    return first.reshape((4,) + first.shape[2:]), second.reshape((4,) + second.shape[2:])


def scatter_dp(value, at):
    rows, width = value.shape[0] // 64, value.shape[1]
    value = value.reshape(2, 2, 4, 4, rows, width)
    got = permute(pick(value, 1 - at["c"]), flip("c", 1))
    value = pick(value, at["c"]) + got
    first, second = scatter_ring(value[0], value[1], "x", at["x"])
    return scatter_ring(first, second, "h", at["h"])


def gather_dp(first, second, at):
    first, second = gather_ring(first, second, "h", at["h"])
    first, second = gather_ring(first, second, "x", at["x"])
    value = jnp.stack([first, second])
    got = permute(value, flip("c", 1))
    value = join(value, got, at["c"])
    return value.reshape(-1, value.shape[-1])


def scatter_tensor(value):
    parts = lax.all_to_all(value.reshape((8, 32) + value.shape[1:]), "tensor", 0, 0, tiled=True)
    return jnp.sum(parts, axis=0)


def gather_tensor(own, at):
    out = jnp.zeros((8,) + own.shape, own.dtype)
    out = lax.dynamic_update_index_in_dim(out, own, at["y"] * 2 + at["l"], 0)
    for dy, dl in ((2, 0), (2, 1), (1, 1), (3, 1), (1, 0), (3, 0), (0, 1)):
        got = permute(own, lambda p: {"y": (p["y"] + dy) % 4, "l": p["l"] ^ dl})
        out = lax.dynamic_update_index_in_dim(
            out, got, ((at["y"] - dy) % 4) * 2 + (at["l"] ^ dl), 0
        )
    return out.reshape((-1,) + own.shape[1:])


def local(
    tokens,
    segment_ids,
    queries,
    teacher_keys,
    teacher_values,
    down_weight,
    rope_weight,
    key_up,
    value_up,
):
    f32 = jnp.float32
    bf16 = jnp.bfloat16
    token_rows = tokens[0]
    segments_row = segment_ids[0]
    seq_len = token_rows.shape[0]
    heads_local = queries.shape[2] // HEAD
    kv_local = teacher_keys.shape[2] // HEAD
    group_size = heads_local // kv_local
    nope_width = HEAD - ROPE
    score_scale = 1.0 / math.sqrt(HEAD)
    contract_cols = (((1,), (1,)), ((), ()))
    contract_rows = (((0,), (0,)), ((), ()))
    positions = doc_positions(segments_row)
    cos_full, sin_full = angle_tables(positions, HEAD)
    cos_rope, sin_rope = angle_tables(positions, ROPE)
    at = coords()
    latent = down_weight.shape[1]
    entry = jnp.concatenate([down_weight, rope_weight.T], axis=1)
    part = jnp.dot(token_rows, entry, preferred_element_type=f32)
    whole = gather_tensor(scatter_tensor(part), at)
    latent_raw, rope_sum = whole[:, :latent], whole[:, latent:].T
    inv_rms = lax.rsqrt(jnp.mean(latent_raw * latent_raw, axis=-1, keepdims=True) + norm_eps)
    normed = latent_raw * inv_rms
    latent_low = normed.astype(bf16)
    rope_key = rotate_rows(rope_sum, cos_rope.T, sin_rope.T).astype(bf16)
    head_queries = queries[0].reshape(seq_len, heads_local, HEAD).transpose(1, 0, 2)
    teacher_q = (
        rotate_last(head_queries.astype(f32), cos_full, sin_full)
        .astype(bf16)
        .reshape(kv_local, group_size, seq_len, HEAD)
    )
    teacher_k = rotate_last(
        teacher_keys[0].reshape(seq_len, kv_local, HEAD).transpose(1, 0, 2).astype(f32),
        cos_full,
        sin_full,
    ).astype(bf16)
    teacher_v = teacher_values[0].reshape(seq_len, kv_local, HEAD).transpose(1, 0, 2)
    key_nope = (
        jnp.dot(latent_low, key_up, preferred_element_type=f32)
        .astype(bf16)
        .reshape(seq_len, heads_local, nope_width)
        .transpose(1, 0, 2)
    )
    head_values = (
        jnp.dot(latent_low, value_up, preferred_element_type=f32)
        .astype(bf16)
        .reshape(seq_len, heads_local, HEAD)
        .transpose(1, 0, 2)
    )
    rotated_q = rotate_last(head_queries[..., :ROPE].astype(f32), cos_rope, sin_rope).astype(bf16)
    student_q = jnp.concatenate([head_queries[..., ROPE:], rotated_q], axis=-1)
    student_k = jnp.concatenate(
        [key_nope, jnp.broadcast_to(rope_key.T[None], (heads_local, seq_len, ROPE))], axis=-1
    )
    block_rows = min(seq_len, 512)
    block_count = seq_len // block_rows

    def attend_block(carry, block_index):
        value_acc, key_acc = carry
        row_start = block_index * block_rows
        doc_mask = block_mask(segments_row, segments_row, row_start)
        teacher_scores = (
            jnp.einsum("kgqd,kpd->kgqp", teacher_q, teacher_k, preferred_element_type=f32)
            * score_scale
        )
        teacher_weights = masked_softmax(teacher_scores, doc_mask).astype(bf16)
        teacher_out = jnp.einsum(
            "kgqp,kpd->kgqd", teacher_weights, teacher_v, preferred_element_type=f32
        ).reshape(heads_local, block_rows, HEAD)
        student_scores = (
            jnp.einsum("hqd,hpd->hqp", student_q, student_k, preferred_element_type=f32)
            * score_scale
        )
        student_weights = masked_softmax(student_scores, doc_mask)
        student_low = student_weights.astype(bf16)
        student_out = jnp.einsum(
            "hqp,hpd->hqd", student_low, head_values, preferred_element_type=f32
        )
        out_grad = (student_out - teacher_out).astype(bf16)
        weight_grad = jnp.einsum("hqd,hpd->hqp", out_grad, head_values, preferred_element_type=f32)
        row_dot = jnp.sum(student_weights * weight_grad, axis=-1, keepdims=True)
        score_grad = (student_weights * (weight_grad - row_dot) * score_scale).astype(bf16)
        value_acc = value_acc + jnp.einsum(
            "hqp,hqd->hpd", student_low, out_grad, preferred_element_type=f32
        )
        key_acc = key_acc + jnp.einsum(
            "hqp,hqd->hpd", score_grad, student_q, preferred_element_type=f32
        )
        return ((value_acc, key_acc), None)

    zeros_acc = jnp.zeros((heads_local, seq_len, HEAD), f32)
    accums, unused = lax.scan(
        attend_block, (zeros_acc, zeros_acc), jnp.arange(block_count, dtype=jnp.int32)
    )
    value_acc, key_acc = accums
    value_flat = value_acc.astype(bf16).transpose(1, 0, 2).reshape(seq_len, heads_local * HEAD)
    nope_grad = (
        key_acc[..., :nope_width]
        .astype(bf16)
        .transpose(1, 0, 2)
        .reshape(seq_len, heads_local * nope_width)
    )
    rope_grad_part = jnp.sum(key_acc[..., nope_width:], axis=0).T
    norm_grad_part = lax.dot_general(
        nope_grad, key_up, contract_cols, preferred_element_type=f32
    ) + lax.dot_general(value_flat, value_up, contract_cols, preferred_element_type=f32)
    up_grads = jnp.concatenate([nope_grad, value_flat], axis=1)
    grad_up = lax.dot_general(latent_low, up_grads, contract_rows, preferred_element_type=f32)
    up_first, up_second = scatter_dp(grad_up, at)
    summed = scatter_tensor(jnp.concatenate([norm_grad_part, rope_grad_part.T], axis=1))
    whole = gather_tensor(summed, at)
    norm_grad, rope_grad_sum = whole[:, :latent], whole[:, latent:].T
    latent_grad = (
        (norm_grad - normed * jnp.mean(norm_grad * normed, axis=-1, keepdims=True)) * inv_rms
    ).astype(bf16)
    rope_grad = unrotate_rows(rope_grad_sum, cos_rope.T, sin_rope.T).astype(bf16)
    entry_grads = jnp.concatenate([latent_grad, rope_grad.T], axis=1)
    grad_entry = lax.dot_general(
        token_rows, entry_grads, contract_rows, preferred_element_type=f32
    )
    first, second = scatter_dp(grad_entry, at)
    grad_up = gather_dp(up_first, up_second, at)
    grad_entry = gather_dp(first, second, at)
    wide = key_up.shape[1]
    return (
        grad_entry[:, :latent],
        grad_entry[:, latent:].T,
        grad_up[:, :wide],
        grad_up[:, wide:],
    )


def solution(mesh):
    in_specs = (
        P("dp", None, "tensor"),
        P("dp", None),
        P("dp", None, "tensor"),
        P("dp", None, "tensor"),
        P("dp", None, "tensor"),
        P("tensor", None),
        P(None, "tensor"),
        P(None, "tensor"),
        P(None, "tensor"),
    )
    out_specs = (P("tensor", None), P(None, "tensor"), P(None, "tensor"), P(None, "tensor"))
    return jax.shard_map(local, mesh=mesh, in_specs=in_specs, out_specs=out_specs, check_vma=False)
```

```python
import math

import jax
import jax.numpy as jnp
from jax import lax
from jax.experimental import pallas as pl
from jax.experimental.pallas import tpu as pltpu
from jax.sharding import PartitionSpec as P


HEAD = 128
ROPE = 64
SEQ = 256
LATENT = 512
THETA = 500000.0
EPS = 1e-06
AXES = ("dp", "tensor")
F32 = jnp.float32
BF16 = jnp.bfloat16

NT = (((1,), (1,)), ((), ()))
TN = (((0,), (0,)), ((), ()))
PACKED = 144


def dot(a, b):
    return jnp.dot(a, b, preferred_element_type=F32)


def dot_nt(a, b):
    return lax.dot_general(a, b, NT, preferred_element_type=F32)


def dot_tn(a, b):
    return lax.dot_general(a, b, TN, preferred_element_type=F32)


def call(body, outs, *args, scalars=0, scratch=(), flops=0):
    spec = pl.BlockSpec(memory_space=pltpu.VMEM)
    smem = pl.BlockSpec(memory_space=pltpu.SMEM)
    size = sum(a.size * a.dtype.itemsize for a in args)
    size += sum(math.prod(o.shape) * o.dtype.itemsize for o in outs)
    return pl.pallas_call(
        body,
        out_shape=outs,
        in_specs=[smem] * scalars + [spec] * (len(args) - scalars),
        out_specs=[spec] * len(outs),
        scratch_shapes=list(scratch),
        compiler_params=pltpu.CompilerParams(vmem_limit_bytes=20 << 20),
        cost_estimate=pl.CostEstimate(flops=flops, bytes_accessed=size, transcendentals=0),
    )(*args)


def shape(*dims, dtype=F32):
    return jax.ShapeDtypeStruct(dims, dtype)


def low_lanes(rows):
    return lax.broadcasted_iota(jnp.int32, (rows, 128), 1) < 64


def pack_rest(first, second):
    return jnp.where(low_lanes(16), first, pltpu.roll(second, 64, 1))


def swap(value):
    lane = lax.broadcasted_iota(jnp.int32, value.shape, 1)
    return jnp.where(lane < 32, pltpu.roll(value, 96, 1), pltpu.roll(value, 32, 1))


def pack(out, k, rows, wide, rest):
    for j in range(4):
        out[k, 32 * j : 32 * j + 32, :] = wide[rows : rows + 32, 128 * j : 128 * j + 128]
    out[k, 128:PACKED, :] = pack_rest(rest[rows : rows + 16], rest[rows + 16 : rows + 32])


def unpack_rest(value, out, rows):
    out[rows : rows + 16, :] = value
    out[rows + 16 : rows + 32, :] = pltpu.roll(value, 64, 1)


def unpack(packed, wide, rest):
    for k in range(8):
        for j in range(4):
            wide[32 * k : 32 * k + 32, 128 * j : 128 * j + 128] = packed[
                k, 32 * j : 32 * j + 32, :
            ].astype(wide.dtype)
        unpack_rest(packed[k, 128:PACKED, :], rest, 32 * k)


def entry_kernel(tokens, down, rope, out):
    wide = dot(tokens[...], down[...])
    rest = dot_nt(tokens[...], rope[...])
    rest = jnp.concatenate([rest, jnp.zeros_like(rest)], axis=1)
    for k in range(8):
        pack(out, k, 32 * k, wide, rest)


def norm_kernel(parts, out, normed_out, inv_out):
    total = jnp.sum(parts[...], axis=0)
    square = jnp.zeros((32, 1), F32)
    for j in range(4):
        tile = total[32 * j : 32 * j + 32]
        square = square + jnp.sum(tile * tile, axis=1, keepdims=True)
    inv = lax.rsqrt(square * (1.0 / LATENT) + EPS)
    inv = jnp.broadcast_to(inv, (32, 128))
    inv_out[...] = inv
    normed = total[:128] * jnp.concatenate([inv] * 4, axis=0)
    normed_out[...] = normed
    for k in range(8):
        out[k, :128, :] = normed
        out[k, 128:, :] = total[128:]


def norm_grad_kernel(at, parts, normed, inv, table, out):
    total = jnp.sum(parts[...], axis=0)
    rows = pl.ds(pl.multiple_of(at[3] * 32, 32), 32)
    rest = jnp.concatenate([total[128:], pltpu.roll(total[128:], 64, 1)], axis=0)
    rest = rest * table[rows, 256:384] - swap(rest) * table[rows, 384:512]
    rest = pack_rest(rest[:16], rest[16:])
    grad = total[:128]
    product = grad * normed[...]
    mean = jnp.zeros((32, 1), F32)
    for j in range(4):
        mean = mean + jnp.sum(product[32 * j : 32 * j + 32], axis=1, keepdims=True)
    mean = jnp.broadcast_to(mean * (1.0 / LATENT), (32, 128))
    four = lambda v: jnp.concatenate([v] * 4, axis=0)
    grad = (grad - normed[...] * four(mean)) * four(inv[...])
    for k in range(8):
        out[k, :128, :] = grad
        out[k, 128:, :] = rest


def seen(seg_col, seg_row):
    i = lax.broadcasted_iota(jnp.int32, (SEQ, SEQ), 0)
    j = lax.broadcasted_iota(jnp.int32, (SEQ, SEQ), 1)
    return (seg_col == seg_row) & (j <= i)


def softmax(scores, mask):
    scores = jnp.where(mask, scores * (1.0 / math.sqrt(HEAD)), -3e38)
    weights = jnp.exp(scores - jnp.max(scores, axis=1, keepdims=True))
    return weights * (1.0 / jnp.sum(weights, axis=1, keepdims=True))


def lanes(h):
    return pl.ds(pl.multiple_of(h * 128, 128), 128)


def teacher_kernel(
    at, queries, keys, values, table, seg_col, seg_row, tokens, out, tokens_keep, tokens_send
):
    mask = seen(seg_col[...], seg_row[...])
    cos, sin = table[:, :128], table[:, 128:256]
    turn = lambda v: (v * cos + pltpu.roll(v, 64, 1) * sin).astype(BF16)
    key = turn(keys[...].astype(F32))
    value = values[...]

    def pair(p, carry):
        for h in (2 * p, 2 * p + 1):
            query = turn(queries[:, lanes(h)].astype(F32))
            weights = softmax(dot_nt(query, key), mask).astype(BF16)
            out[:, lanes(h)] = dot(weights, value)
        return carry

    lax.fori_loop(0, 4, pair, 0)
    half = lambda c: tokens[:, pl.ds(pl.multiple_of(c * 512, 512), 512)].T
    tokens_keep[...] = half(at[0])
    tokens_send[...] = half(1 - at[0]).astype(F32)


def student_kernel(
    at, packed, queries, key_up, value_up, teacher, table, seg_col, seg_row,
    grads_keep, grads_send, norm_out, latent, rest, nope, head_values, rest_sum, grads_out,
):
    unpack(packed, latent, rest)
    cos, sin = table[:, 256:384], table[:, 384:512]
    low = low_lanes(SEQ)
    turn = lambda v: v * cos + swap(v) * sin
    rope_key = turn(rest[...])
    nope[...] = dot(latent[...], key_up[...])
    head_values[...] = dot(latent[...], value_up[...]).astype(BF16)
    mask = seen(seg_col[...], seg_row[...])
    scale = 1.0 / math.sqrt(HEAD)
    rest_sum[...] = jnp.zeros_like(rest_sum)

    def head(h, key_part):
        query = turn(queries[:, lanes(h)].astype(F32)).astype(BF16)
        key = jnp.where(low, rope_key, key_part).astype(BF16)
        weights = softmax(dot_nt(query, key), mask)
        weights_low = weights.astype(BF16)
        value = head_values[:, lanes(h)]
        out_grad = (dot(weights_low, value) - teacher[:, lanes(h)]).astype(BF16)
        weight_grad = dot_nt(out_grad, value)
        row = jnp.sum(weights * weight_grad, axis=1, keepdims=True)
        score_grad = (weights * (weight_grad - row) * scale).astype(BF16)
        grads_out[:, lanes(4 + h)] = dot_tn(weights_low, out_grad).astype(BF16)
        return dot_tn(score_grad, query)

    def pair(p, carry):
        both = nope[:, lanes(p)]
        first = head(2 * p, pltpu.roll(both, 64, 1))
        second = head(2 * p + 1, both)
        rest_sum[...] += first + second
        grads_out[:, lanes(p)] = jnp.where(low, pltpu.roll(first, 64, 1), second).astype(BF16)
        return carry

    lax.fori_loop(0, 4, pair, 0)
    wide = dot_nt(grads_out[:, :512], key_up[...]) + dot_nt(grads_out[:, 512:], value_up[...])
    rest_all = rest_sum[...]
    for ref, c in ((grads_keep, at[0]), (grads_send, 1 - at[0])):
        keys = pl.ds(pl.multiple_of(c * 256, 256), 256)
        values = pl.ds(pl.multiple_of(512 + c * 512, 512), 512)
        ref[:, :256] = grads_out[:, keys].astype(ref.dtype)
        ref[:, 256:] = grads_out[:, values].astype(ref.dtype)
    for k in range(8):
        pack(norm_out, k, 32 * k, wide, rest_all)


def up_kernel(at, packed, other_packed, grads, other_grads, *outs):
    *outs, latent, rest = outs
    unpack(packed, latent, rest)
    whole = dot_tn(latent[...], grads[...])
    unpack(other_packed, latent, rest)
    whole = whole + dot_tn(latent[...], other_grads[...].astype(BF16))
    for quarter in range(4):
        for step in range(4):
            @pl.when((at[1] + step) % 4 == quarter)
            def _(quarter=quarter, step=step):
                outs[step][...] = whole[128 * quarter : 128 * quarter + 128]


def split_kernel(at, own, first, second, third, *outs):
    for step in range(4):
        rows = pl.ds(pl.multiple_of((at[2] + step) % 4 * 32, 32), 32)
        outs[step][...] = (own[rows, :] + first[rows, :]) + (second[rows, :] + third[rows, :])


def entry_grad_kernel(packed, other_packed, tokens, other_tokens, out, grads, rest):
    unpack(packed, grads, rest)
    grads[:, 512:] = jnp.where(low_lanes(SEQ), rest[...], 0.0).astype(BF16)
    whole = dot(tokens[...], grads[...])
    unpack(other_packed, grads, rest)
    grads[:, 512:] = jnp.where(low_lanes(SEQ), rest[...], 0.0).astype(BF16)
    whole = whole + dot(other_tokens[...].astype(BF16), grads[...])
    for k in range(16):
        pack(out, k, 32 * k, whole[:, :512], whole[:, 512:])


def up_out_kernel(at, *refs):
    *parts, key_out, value_out = refs
    for c in range(2):
        column = jnp.where(c == 0, at[0], 1 - at[0])
        keys = pl.ds(pl.multiple_of(column * 256, 256), 256)
        values = pl.ds(pl.multiple_of(column * 512, 512), 512)
        for step in range(4):
            ref = parts[4 * c + step]
            for depth in range(4):
                block = (at[1] - step + 4) % 4 * 4 + (at[2] - depth + 4) % 4
                rows = pl.ds(pl.multiple_of(block * 32, 32), 32)
                key_out[rows, keys] = ref[depth, :, :256]
                value_out[rows, values] = ref[depth, :, 256:]


def entry_out_kernel(at, own, other, down_out, rope_out, rest):
    c = at[0]
    for half, ref in ((c, own), (1 - c, other)):
        def group(g, carry, half=half, ref=ref):
            first = half * 4 + g
            for b in range(4):
                rows = pl.ds(pl.multiple_of(first * 128 + 32 * b, 32), 32)
                for j in range(4):
                    down_out[rows, 128 * j : 128 * j + 128] = ref[
                        4 * g + b, 32 * j : 32 * j + 32, :
                    ]
                unpack_rest(ref[4 * g + b, 128:PACKED, :], rest, 32 * b)
            rope_out[:, lanes(first)] = rest[...].T[:64]
            return carry

        lax.fori_loop(0, 4, group, 0)


def sum_kernel(parts, out):
    out[...] = (parts[0] + parts[1]) + (parts[2] + parts[3])


def sum_spread_kernel(parts, out):
    total = (parts[0] + parts[1]) + (parts[2] + parts[3])
    for k in range(4):
        out[k] = total


def spread_kernel(value, out):
    for k in range(4):
        out[k] = value[...]


def permute(value, move):
    pairs = []
    for i in range(256):
        d, t = divmod(i, 8)
        at = dict(x=d // 8, h=(d // 2) % 4, c=d % 2, y=t // 2, l=t % 2)
        to = {**at, **move(at)}
        j = (to["x"] * 8 + to["h"] * 2 + to["c"]) * 8 + to["y"] * 2 + to["l"]
        pairs.append((i, j))
    return lax.ppermute(value, AXES, pairs)


def other_core(value):
    return permute(value, lambda at: {"c": 1 - at["c"]})


def around(value, axis):
    values = value if isinstance(value, list) else [value] * 3
    moves = [lambda at, k=k: {axis: (at[axis] + k) % 4} for k in (1, 2, 3)]
    return [permute(v, move) for v, move in zip(values, moves)]


X_GROUPS = [[8 * x + r for x in range(4)] for r in range(8)]
H_GROUPS = [[8 * x + 2 * h + c for h in range(4)] for x in range(4) for c in range(2)]


def exchange(parts, groups=None):
    axis = "tensor" if groups is None else "dp"
    return lax.all_to_all(parts, axis, 0, 0, axis_index_groups=groups, tiled=True)


def tables(segments):
    index = jnp.arange(SEQ, dtype=jnp.int32)
    start = jnp.sum((segments[None, :] < segments[:, None]).astype(jnp.int32), axis=1)
    position = (index - start).astype(F32)

    def angles(width):
        exponent = jnp.arange(width // 2, dtype=F32) * (2.0 / width)
        return position[:, None] * jnp.exp(-exponent * jnp.log(F32(THETA)))[None, :]

    full, part = angles(HEAD), angles(ROPE)
    cos, sin = jnp.cos(full), jnp.sin(full)
    cos_part, sin_part = jnp.cos(part), jnp.sin(part)
    one, zero = jnp.ones((SEQ, 64), F32), jnp.zeros((SEQ, 64), F32)
    return jnp.concatenate(
        [cos, cos, -sin, sin, cos_part, cos_part, one, -sin_part, sin_part, zero], axis=1
    )


def local(tokens, segment_ids, queries, keys, values, down, rope, key_up, value_up):
    tokens, segments, queries = tokens[0], segment_ids[0], queries[0]
    d = lax.axis_index("dp")
    at = jnp.stack([d % 2, d // 8, d // 2 % 4, lax.axis_index("tensor")])
    seg_col, seg_row = segments[:, None], segments[None, :]
    chunks = shape(8, PACKED, 128)
    unpacked = [pltpu.VMEM((SEQ, LATENT), BF16), pltpu.VMEM((SEQ, 128), F32)]

    (part,) = call(entry_kernel, [chunks], tokens, down, rope, flops=2 * 256 * 1024 * 576)
    parts = exchange(part)
    table = tables(segments)
    teacher, tokens_keep, tokens_send = call(
        teacher_kernel,
        [shape(SEQ, 1024), shape(512, SEQ, dtype=BF16), shape(512, SEQ)],
        at, queries, keys[0], values[0], table, seg_col, seg_row, tokens,
        scalars=1, flops=4 * 8 * 256 * 256 * 128,
    )
    tokens_other = other_core(tokens_send)
    parts, teacher = lax.optimization_barrier((parts, teacher))
    replicas, normed, inv = call(norm_kernel, [chunks, shape(128, 128), shape(32, 128)], parts)
    packed = exchange(replicas)
    packed_other = other_core(packed)
    grads_keep, grads_send, part = call(
        student_kernel,
        [shape(SEQ, 768, dtype=BF16), shape(SEQ, 768), chunks],
        at, packed, queries, key_up, value_up, teacher, table, seg_col, seg_row,
        scalars=1,
        scratch=unpacked + [
            pltpu.VMEM((SEQ, 512), F32),
            pltpu.VMEM((SEQ, 1024), BF16),
            pltpu.VMEM((SEQ, 128), F32),
            pltpu.VMEM((SEQ, 1536), BF16),
        ],
        flops=10 * 8 * 256 * 256 * 128,
    )
    grads_other = other_core(grads_send)
    parts = exchange(part)
    quarters = call(
        up_kernel, [shape(128, 768)] * 4, at, packed, packed_other, grads_keep, grads_other,
        scalars=1, scratch=unpacked, flops=2 * 512 * 512 * 768,
    )
    received = around(list(quarters[1:]), "x")
    (replicas,) = call(norm_grad_kernel, [chunks], at, parts, normed, inv, table, scalars=1)
    packed = exchange(replicas)
    packed_other = other_core(packed)
    (entry,) = call(
        entry_grad_kernel, [shape(16, PACKED, 128)],
        packed, packed_other, tokens_keep, tokens_other,
        scratch=[pltpu.VMEM((SEQ, 640), BF16), pltpu.VMEM((SEQ, 128), F32)],
        flops=2 * 512 * 512 * 640,
    )
    entry = exchange(entry.reshape(4, 4, PACKED, 128), X_GROUPS)
    quarters = call(split_kernel, [shape(32, 768)] * 4, at, quarters[0], *received, scalars=1)
    received = around(list(quarters[1:]), "h")
    (entry,) = call(sum_kernel, [shape(4, PACKED, 128)], entry)
    entry = exchange(entry, H_GROUPS)
    up = (quarters[0] + received[0]) + (received[1] + received[2])
    up_all = jnp.stack([up] + around(up, "h"))
    (entry,) = call(sum_spread_kernel, [shape(4, PACKED, 128)], entry)
    entry = exchange(entry, H_GROUPS)
    received = [up_all] + around(up_all, "x")
    (entry,) = call(spread_kernel, [shape(4, 4, PACKED, 128)], entry)
    entry = exchange(entry, X_GROUPS).reshape(16, PACKED, 128)
    others = [other_core(v) for v in received]
    grad_key, grad_value = call(
        up_out_kernel, [shape(512, 512), shape(512, 1024)], at, *received, *others, scalars=1,
    )
    entry_other = other_core(entry)
    grad_down, grad_rope = call(
        entry_out_kernel, [shape(1024, 512), shape(64, 1024)], at, entry, entry_other,
        scalars=1, scratch=[pltpu.VMEM((128, 128), F32)],
    )
    return grad_down, grad_rope, grad_key, grad_value


def solution(mesh):
    token = P("dp", None, "tensor")
    rows, columns = P("tensor", None), P(None, "tensor")
    in_specs = (token, P("dp", None), token, token, token, rows, columns, columns, columns)
    out_specs = (rows, columns, columns, columns)
    return jax.shard_map(local, mesh=mesh, in_specs=in_specs, out_specs=out_specs, check_vma=False)
```

```python
import functools
import math

import jax
import jax.numpy as jnp
from jax import lax
from jax.experimental import pallas as pl
from jax.experimental.pallas import tpu as pltpu
from jax.sharding import PartitionSpec as P


HEAD = 128
ROPE = 64
SEQ = 256
LATENT = 512
THETA = 500000.0
EPS = 1e-06
AXES = ("dp", "tensor")
F32 = jnp.float32
BF16 = jnp.bfloat16

NT = (((1,), (1,)), ((), ()))
TN = (((0,), (0,)), ((), ()))
PACKED = 144


def dot(a, b):
    return jnp.dot(a, b, preferred_element_type=F32)


def dot_nt(a, b):
    return lax.dot_general(a, b, NT, preferred_element_type=F32)


def dot_tn(a, b):
    return lax.dot_general(a, b, TN, preferred_element_type=F32)


def call(body, outs, *args, scalars=0, scratch=(), flops=0, mib=20, aliases=None):
    spec = pl.BlockSpec(memory_space=pltpu.VMEM)
    smem = pl.BlockSpec(memory_space=pltpu.SMEM)
    anywhere = pl.BlockSpec(memory_space=pl.ANY)
    specs = [smem] * scalars + [spec] * (len(args) - scalars)
    for k in aliases or {}:
        specs[k] = anywhere
    size = sum(a.size * a.dtype.itemsize for a in args)
    size += sum(math.prod(o.shape) * o.dtype.itemsize for o in outs)
    return pl.pallas_call(
        body,
        out_shape=outs,
        in_specs=specs,
        out_specs=[anywhere if aliases is not None else spec] * len(outs),
        scratch_shapes=list(scratch),
        input_output_aliases=aliases or {},
        compiler_params=pltpu.CompilerParams(vmem_limit_bytes=mib << 20),
        cost_estimate=pl.CostEstimate(flops=flops, bytes_accessed=size, transcendentals=0),
    )(*args)


def shape(*dims, dtype=F32):
    return jax.ShapeDtypeStruct(dims, dtype)


def low_lanes(rows):
    return lax.broadcasted_iota(jnp.int32, (rows, 128), 1) < 64


def pack_rest(first, second):
    return jnp.where(low_lanes(16), first, pltpu.roll(second, 64, 1))


def swap(value):
    lane = lax.broadcasted_iota(jnp.int32, value.shape, 1)
    return jnp.where(lane < 32, pltpu.roll(value, 96, 1), pltpu.roll(value, 32, 1))


def pack(out, k, rows, wide, rest):
    for j in range(4):
        out[k, 32 * j : 32 * j + 32, :] = wide[rows : rows + 32, 128 * j : 128 * j + 128]
    out[k, 128:PACKED, :] = pack_rest(rest[rows : rows + 16], rest[rows + 16 : rows + 32])


def unpack_rest(value, out, rows):
    out[rows : rows + 16, :] = value
    out[rows + 16 : rows + 32, :] = pltpu.roll(value, 64, 1)


def unpack(packed, wide, rest):
    for k in range(8):
        for j in range(4):
            wide[32 * k : 32 * k + 32, 128 * j : 128 * j + 128] = packed[
                k, 32 * j : 32 * j + 32, :
            ].astype(wide.dtype)
        unpack_rest(packed[k, 128:PACKED, :], rest, 32 * k)


def entry_kernel(tokens, down, rope, out):
    wide = dot(tokens[...], down[...])
    rest = dot_nt(tokens[...], rope[...])
    rest = jnp.concatenate([rest, jnp.zeros_like(rest)], axis=1)
    for k in range(8):
        pack(out, k, 32 * k, wide, rest)


def norm_kernel(parts, out, normed_out, inv_out):
    total = jnp.sum(parts[...], axis=0)
    square = jnp.zeros((32, 1), F32)
    for j in range(4):
        tile = total[32 * j : 32 * j + 32]
        square = square + jnp.sum(tile * tile, axis=1, keepdims=True)
    inv = lax.rsqrt(square * (1.0 / LATENT) + EPS)
    inv = jnp.broadcast_to(inv, (32, 128))
    inv_out[...] = inv
    normed = total[:128] * jnp.concatenate([inv] * 4, axis=0)
    normed_out[...] = normed
    for k in range(8):
        out[k, :128, :] = normed
        out[k, 128:, :] = total[128:]


def norm_grad_kernel(at, parts, normed, inv, table, out):
    total = jnp.sum(parts[...], axis=0)
    rows = pl.ds(pl.multiple_of(at[3] * 32, 32), 32)
    rest = jnp.concatenate([total[128:], pltpu.roll(total[128:], 64, 1)], axis=0)
    rest = rest * table[rows, 256:384] - swap(rest) * table[rows, 384:512]
    rest = pack_rest(rest[:16], rest[16:])
    grad = total[:128]
    product = grad * normed[...]
    mean = jnp.zeros((32, 1), F32)
    for j in range(4):
        mean = mean + jnp.sum(product[32 * j : 32 * j + 32], axis=1, keepdims=True)
    mean = jnp.broadcast_to(mean * (1.0 / LATENT), (32, 128))
    four = lambda v: jnp.concatenate([v] * 4, axis=0)
    grad = (grad - normed[...] * four(mean)) * four(inv[...])
    for k in range(8):
        out[k, :128, :] = grad
        out[k, 128:, :] = rest


def seen(seg_col, seg_row):
    i = lax.broadcasted_iota(jnp.int32, (SEQ, SEQ), 0)
    j = lax.broadcasted_iota(jnp.int32, (SEQ, SEQ), 1)
    return (seg_col == seg_row) & (j <= i)


def softmax(scores, mask):
    scores = jnp.where(mask, scores * (1.0 / math.sqrt(HEAD)), -3e38)
    weights = jnp.exp(scores - jnp.max(scores, axis=1, keepdims=True))
    return weights * (1.0 / jnp.sum(weights, axis=1, keepdims=True))


def lanes(h):
    return pl.ds(pl.multiple_of(h * 128, 128), 128)


def teacher_kernel(
    at, queries, keys, values, table, seg_col, seg_row, tokens, out, tokens_keep, tokens_send
):
    mask = seen(seg_col[...], seg_row[...])
    cos, sin = table[:, :128], table[:, 128:256]
    turn = lambda v: (v * cos + pltpu.roll(v, 64, 1) * sin).astype(BF16)
    key = turn(keys[...].astype(F32))
    value = values[...]

    def pair(p, carry):
        for h in (2 * p, 2 * p + 1):
            query = turn(queries[:, lanes(h)].astype(F32))
            weights = softmax(dot_nt(query, key), mask).astype(BF16)
            out[:, lanes(h)] = dot(weights, value)
        return carry

    lax.fori_loop(0, 4, pair, 0)
    half = lambda c: tokens[:, pl.ds(pl.multiple_of(c * 512, 512), 512)].T
    tokens_keep[...] = half(at[0])
    tokens_send[...] = half(1 - at[0]).astype(F32)


def student_kernel(
    at, packed, queries, key_up, value_up, teacher, table, seg_col, seg_row,
    grads_keep, grads_send, norm_out, latent, rest, nope, head_values, rest_sum, grads_out,
):
    unpack(packed, latent, rest)
    cos, sin = table[:, 256:384], table[:, 384:512]
    low = low_lanes(SEQ)
    turn = lambda v: v * cos + swap(v) * sin
    rope_key = turn(rest[...])
    nope[...] = dot(latent[...], key_up[...])
    head_values[...] = dot(latent[...], value_up[...]).astype(BF16)
    mask = seen(seg_col[...], seg_row[...])
    scale = 1.0 / math.sqrt(HEAD)
    rest_sum[...] = jnp.zeros_like(rest_sum)

    def head(h, key_part):
        query = turn(queries[:, lanes(h)].astype(F32)).astype(BF16)
        key = jnp.where(low, rope_key, key_part).astype(BF16)
        weights = softmax(dot_nt(query, key), mask)
        weights_low = weights.astype(BF16)
        value = head_values[:, lanes(h)]
        out_grad = (dot(weights_low, value) - teacher[:, lanes(h)]).astype(BF16)
        weight_grad = dot_nt(out_grad, value)
        row = jnp.sum(weights * weight_grad, axis=1, keepdims=True)
        score_grad = (weights * (weight_grad - row) * scale).astype(BF16)
        grads_out[:, lanes(4 + h)] = dot_tn(weights_low, out_grad).astype(BF16)
        return dot_tn(score_grad, query)

    def pair(p, carry):
        both = nope[:, lanes(p)]
        first = head(2 * p, pltpu.roll(both, 64, 1))
        second = head(2 * p + 1, both)
        rest_sum[...] += first + second
        grads_out[:, lanes(p)] = jnp.where(low, pltpu.roll(first, 64, 1), second).astype(BF16)
        return carry

    lax.fori_loop(0, 4, pair, 0)
    wide = dot_nt(grads_out[:, :512], key_up[...]) + dot_nt(grads_out[:, 512:], value_up[...])
    rest_all = rest_sum[...]
    for ref, c in ((grads_keep, at[0]), (grads_send, 1 - at[0])):
        keys = pl.ds(pl.multiple_of(c * 256, 256), 256)
        values = pl.ds(pl.multiple_of(512 + c * 512, 512), 512)
        ref[:, :256] = grads_out[:, keys].astype(ref.dtype)
        ref[:, 256:] = grads_out[:, values].astype(ref.dtype)
    for k in range(8):
        pack(norm_out, k, 32 * k, wide, rest_all)


def up_kernel(at, packed, other_packed, grads, other_grads, *outs):
    *outs, latent, rest = outs
    unpack(packed, latent, rest)
    whole = dot_tn(latent[...], grads[...])
    unpack(other_packed, latent, rest)
    whole = whole + dot_tn(latent[...], other_grads[...].astype(BF16))
    for quarter in range(4):
        for step in range(4):
            @pl.when((at[1] + step) % 4 == quarter)
            def _(quarter=quarter, step=step):
                outs[step][...] = whole[128 * quarter : 128 * quarter + 128]


def split_kernel(at, own, first, second, third, *outs):
    for step in range(4):
        rows = pl.ds(pl.multiple_of((at[2] + step) % 4 * 32, 32), 32)
        outs[step][...] = (own[rows, :] + first[rows, :]) + (second[rows, :] + third[rows, :])


def entry_grad_kernel(at, packed, other_packed, tokens, other_tokens, *refs):
    *outs, grads, other_grads, rest = refs
    for source, ref in ((packed, grads), (other_packed, other_grads)):
        unpack(source, ref, rest)
        ref[:, 512:] = jnp.where(low_lanes(SEQ), rest[...], 0.0).astype(BF16)
    for step in range(4):
        rows = pl.ds(pl.multiple_of((at[1] + step) % 4 * 128, 128), 128)
        whole = dot(tokens[rows, :], grads[...])
        whole = whole + dot(other_tokens[rows, :].astype(BF16), other_grads[...])
        for k in range(4):
            pack(outs[step], k, 32 * k, whole[:, :512], whole[:, 512:])


def entry_split_kernel(at, own, first, second, third, *outs):
    for step in range(4):
        k = (at[2] + step) % 4
        outs[step][...] = (own[k] + first[k]) + (second[k] + third[k])


def entry_sum_kernel(own, first, second, third, out):
    out[...] = (own[...] + first[...]) + (second[...] + third[...])


def up_out_kernel(at, *refs):
    *parts, key_out, value_out = refs
    for c in range(2):
        column = jnp.where(c == 0, at[0], 1 - at[0])
        keys = pl.ds(pl.multiple_of(column * 256, 256), 256)
        values = pl.ds(pl.multiple_of(column * 512, 512), 512)
        for step in range(4):
            ref = parts[4 * c + step]
            for depth in range(4):
                block = (at[1] - step + 4) % 4 * 4 + (at[2] - depth + 4) % 4
                rows = pl.ds(pl.multiple_of(block * 32, 32), 32)
                key_out[rows, keys] = ref[depth, :, :256]
                value_out[rows, values] = ref[depth, :, 256:]


def entry_out_kernel(own, at, *refs):
    parts, (down_out, rope_out, down, rope, rest, sems) = refs[:4], refs[-6:]
    half = at[0] if own else 1 - at[0]
    for step in range(4):
        first = (at[1] - step + 4) % 4
        for depth in range(4):
            spot = (at[2] - depth + 4) % 4 * 32
            rows = pl.ds(pl.multiple_of(first * 128 + spot, 32), 32)
            for j in range(4):
                down[rows, 128 * j : 128 * j + 128] = parts[step][depth, 32 * j : 32 * j + 32, :]
            value = parts[step][depth, 128:PACKED, :]
            rest[pl.ds(pl.multiple_of(spot, 32), 16), :] = value
            rest[pl.ds(pl.multiple_of(spot + 16, 16), 16), :] = pltpu.roll(value, 64, 1)
        rope[:, lanes(first)] = rest[...].T[:64]
    where = pl.ds(pl.multiple_of(half * 512, 512), 512)
    copies = [
        pltpu.make_async_copy(down, down_out.at[where, :], sems.at[0]),
        pltpu.make_async_copy(rope, rope_out.at[:, where], sems.at[1]),
    ]
    for copy in copies:
        copy.start()
    for copy in copies:
        copy.wait()


def stack_kernel(*refs):
    *parts, out = refs
    for k, part in enumerate(parts):
        out[k] = part[...]


def permute(value, move):
    pairs = []
    for i in range(256):
        d, t = divmod(i, 8)
        at = dict(x=d // 8, h=(d // 2) % 4, c=d % 2, y=t // 2, l=t % 2)
        to = {**at, **move(at)}
        j = (to["x"] * 8 + to["h"] * 2 + to["c"]) * 8 + to["y"] * 2 + to["l"]
        pairs.append((i, j))
    return lax.ppermute(value, AXES, pairs)


def other_core(value):
    return permute(value, lambda at: {"c": 1 - at["c"]})


def around(value, axis):
    values = value if isinstance(value, list) else [value] * 3
    moves = [lambda at, k=k: {axis: (at[axis] + k) % 4} for k in (1, 2, 3)]
    return [permute(v, move) for v, move in zip(values, moves)]


def exchange(parts):
    return lax.all_to_all(parts, "tensor", 0, 0, tiled=True)


def tables(segments):
    index = jnp.arange(SEQ, dtype=jnp.int32)
    start = jnp.sum((segments[None, :] < segments[:, None]).astype(jnp.int32), axis=1)
    position = (index - start).astype(F32)

    def angles(width):
        exponent = jnp.arange(width // 2, dtype=F32) * (2.0 / width)
        return position[:, None] * jnp.exp(-exponent * jnp.log(F32(THETA)))[None, :]

    full, part = angles(HEAD), angles(ROPE)
    cos, sin = jnp.cos(full), jnp.sin(full)
    cos_part, sin_part = jnp.cos(part), jnp.sin(part)
    one, zero = jnp.ones((SEQ, 64), F32), jnp.zeros((SEQ, 64), F32)
    return jnp.concatenate(
        [cos, cos, -sin, sin, cos_part, cos_part, one, -sin_part, sin_part, zero], axis=1
    )


def local(tokens, segment_ids, queries, keys, values, down, rope, key_up, value_up):
    tokens, segments, queries = tokens[0], segment_ids[0], queries[0]
    d = lax.axis_index("dp")
    at = jnp.stack([d % 2, d // 8, d // 2 % 4, lax.axis_index("tensor")])
    seg_col, seg_row = segments[:, None], segments[None, :]
    chunks = shape(8, PACKED, 128)
    unpacked = [pltpu.VMEM((SEQ, LATENT), BF16), pltpu.VMEM((SEQ, 128), F32)]

    (part,) = call(entry_kernel, [chunks], tokens, down, rope, flops=2 * 256 * 1024 * 576, mib=60)
    parts = exchange(part)
    table = tables(segments)
    teacher, tokens_keep, tokens_send = call(
        teacher_kernel,
        [shape(SEQ, 1024), shape(512, SEQ, dtype=BF16), shape(512, SEQ)],
        at, queries, keys[0], values[0], table, seg_col, seg_row, tokens,
        scalars=1, flops=4 * 8 * 256 * 256 * 128, mib=60,
    )
    tokens_other = other_core(tokens_send)
    parts, teacher = lax.optimization_barrier((parts, teacher))
    replicas, normed, inv = call(norm_kernel, [chunks, shape(128, 128), shape(32, 128)], parts)
    packed = exchange(replicas)
    packed_other = other_core(packed)
    grads_keep, grads_send, part = call(
        student_kernel,
        [shape(SEQ, 768, dtype=BF16), shape(SEQ, 768), chunks],
        at, packed, queries, key_up, value_up, teacher, table, seg_col, seg_row,
        scalars=1,
        scratch=unpacked + [
            pltpu.VMEM((SEQ, 512), F32),
            pltpu.VMEM((SEQ, 1024), BF16),
            pltpu.VMEM((SEQ, 128), F32),
            pltpu.VMEM((SEQ, 1536), BF16),
        ],
        flops=10 * 8 * 256 * 256 * 128, mib=60,
    )
    grads_other = other_core(grads_send)
    parts = exchange(part)
    quarters = call(
        up_kernel, [shape(128, 768)] * 4, at, packed, packed_other, grads_keep, grads_other,
        scalars=1, scratch=unpacked, flops=2 * 512 * 512 * 768,
    )
    received = around(list(quarters[1:]), "x")
    (replicas,) = call(norm_grad_kernel, [chunks], at, parts, normed, inv, table, scalars=1)
    packed = exchange(replicas)
    packed_other = other_core(packed)
    quarters = call(split_kernel, [shape(32, 768)] * 4, at, quarters[0], *received, scalars=1)
    received = around(list(quarters[1:]), "h")
    entries = call(
        entry_grad_kernel, [shape(4, PACKED, 128)] * 4,
        at, packed, packed_other, tokens_keep, tokens_other, scalars=1,
        scratch=[pltpu.VMEM((SEQ, 640), BF16)] * 2 + [pltpu.VMEM((SEQ, 128), F32)],
        flops=2 * 512 * 512 * 640,
    )
    arrived = around(list(entries[1:]), "x")
    up = (quarters[0] + received[0]) + (received[1] + received[2])
    (up_all,) = call(stack_kernel, [shape(4, 32, 768)], up, *around(up, "h"))
    entries = call(
        entry_split_kernel, [shape(PACKED, 128)] * 4, at, entries[0], *arrived, scalars=1,
    )
    arrived = around(list(entries[1:]), "h")
    received = [up_all] + around(up_all, "x")
    (entry,) = call(entry_sum_kernel, [shape(PACKED, 128)], entries[0], *arrived)
    entry = jnp.stack([entry] + around(entry, "h"))
    entries = [entry] + around(entry, "x")
    others = [other_core(v) for v in received]
    grad_key, grad_value = call(
        up_out_kernel, [shape(512, 512), shape(512, 1024)], at, *received, *others, scalars=1,
    )
    others = [other_core(v) for v in entries]
    outs = [shape(1024, 512), shape(64, 1024)]
    scratch = [
        pltpu.VMEM((512, 512), F32),
        pltpu.VMEM((64, 512), F32),
        pltpu.VMEM((128, 128), F32),
        pltpu.SemaphoreType.DMA((2,)),
    ]
    halves = call(
        functools.partial(entry_out_kernel, True), outs, at, *entries, scalars=1,
        scratch=scratch, aliases={},
    )
    grad_down, grad_rope = call(
        functools.partial(entry_out_kernel, False), outs, at, *others, *halves, scalars=1,
        scratch=scratch, aliases={5: 0, 6: 1},
    )
    return grad_down, grad_rope, grad_key, grad_value


def solution(mesh):
    token = P("dp", None, "tensor")
    rows, columns = P("tensor", None), P(None, "tensor")
    in_specs = (token, P("dp", None), token, token, token, rows, columns, columns, columns)
    out_specs = (rows, columns, columns, columns)
    return jax.shard_map(local, mesh=mesh, in_specs=in_specs, out_specs=out_specs, check_vma=False)
```

```python
import functools
import math

import jax
import jax.numpy as jnp
from jax import lax
from jax.experimental import pallas as pl
from jax.experimental.pallas import tpu as pltpu
from jax.sharding import PartitionSpec as P


HEAD = 128
ROPE = 64
SEQ = 256
LATENT = 512
THETA = 500000.0
EPS = 1e-06
AXES = ("dp", "tensor")
F32 = jnp.float32
BF16 = jnp.bfloat16

NT = (((1,), (1,)), ((), ()))
TN = (((0,), (0,)), ((), ()))
PACKED = 144


def dot(a, b):
    return jnp.dot(a, b, preferred_element_type=F32)


def dot_nt(a, b):
    return lax.dot_general(a, b, NT, preferred_element_type=F32)


def dot_tn(a, b):
    return lax.dot_general(a, b, TN, preferred_element_type=F32)


def call(body, outs, *args, scalars=0, scratch=(), flops=0, mib=20, aliases=None):
    spec = pl.BlockSpec(memory_space=pltpu.VMEM)
    smem = pl.BlockSpec(memory_space=pltpu.SMEM)
    anywhere = pl.BlockSpec(memory_space=pl.ANY)
    specs = [smem] * scalars + [spec] * (len(args) - scalars)
    for k in aliases or {}:
        specs[k] = anywhere
    size = sum(a.size * a.dtype.itemsize for a in args)
    size += sum(math.prod(o.shape) * o.dtype.itemsize for o in outs)
    return pl.pallas_call(
        body,
        out_shape=outs,
        in_specs=specs,
        out_specs=[anywhere if aliases is not None else spec] * len(outs),
        scratch_shapes=list(scratch),
        input_output_aliases=aliases or {},
        compiler_params=pltpu.CompilerParams(vmem_limit_bytes=mib << 20),
        cost_estimate=pl.CostEstimate(flops=flops, bytes_accessed=size, transcendentals=0),
    )(*args)


def shape(*dims, dtype=F32):
    return jax.ShapeDtypeStruct(dims, dtype)


def low_lanes(rows):
    return lax.broadcasted_iota(jnp.int32, (rows, 128), 1) < 64


def pack_rest(first, second):
    return jnp.where(low_lanes(16), first, pltpu.roll(second, 64, 1))


def swap(value):
    lane = lax.broadcasted_iota(jnp.int32, value.shape, 1)
    return jnp.where(lane < 32, pltpu.roll(value, 96, 1), pltpu.roll(value, 32, 1))


def pack(out, k, rows, wide, rest):
    for j in range(4):
        out[k, 32 * j : 32 * j + 32, :] = wide[rows : rows + 32, 128 * j : 128 * j + 128]
    out[k, 128:PACKED, :] = pack_rest(rest[rows : rows + 16], rest[rows + 16 : rows + 32])


def unpack_rest(value, out, rows):
    out[rows : rows + 16, :] = value
    out[rows + 16 : rows + 32, :] = pltpu.roll(value, 64, 1)


def unpack(packed, wide, rest):
    for k in range(8):
        for j in range(4):
            wide[32 * k : 32 * k + 32, 128 * j : 128 * j + 128] = packed[
                k, 32 * j : 32 * j + 32, :
            ].astype(wide.dtype)
        unpack_rest(packed[k, 128:PACKED, :], rest, 32 * k)


def entry_kernel(tokens, down, rope, out):
    wide = dot(tokens[...], down[...])
    rest = dot_nt(tokens[...], rope[...])
    rest = jnp.concatenate([rest, jnp.zeros_like(rest)], axis=1)
    for k in range(8):
        pack(out, k, 32 * k, wide, rest)


def norm_kernel(parts, out, normed_out, inv_out):
    total = jnp.sum(parts[...], axis=0)
    square = jnp.zeros((32, 1), F32)
    for j in range(4):
        tile = total[32 * j : 32 * j + 32]
        square = square + jnp.sum(tile * tile, axis=1, keepdims=True)
    inv = lax.rsqrt(square * (1.0 / LATENT) + EPS)
    inv = jnp.broadcast_to(inv, (32, 128))
    inv_out[...] = inv
    normed = total[:128] * jnp.concatenate([inv] * 4, axis=0)
    normed_out[...] = normed
    for k in range(8):
        out[k, :128, :] = normed
        out[k, 128:, :] = total[128:]


def norm_grad_kernel(at, parts, normed, inv, cos_part, sin_part, out):
    total = jnp.sum(parts[...], axis=0)
    rows = pl.ds(pl.multiple_of(at[3] * 32, 32), 32)
    rest = jnp.concatenate([total[128:], pltpu.roll(total[128:], 64, 1)], axis=0)
    cos, sin = part_table(cos_part[rows, :], sin_part[rows, :])
    rest = rest * cos - swap(rest) * sin
    rest = pack_rest(rest[:16], rest[16:])
    grad = total[:128]
    product = grad * normed[...]
    mean = jnp.zeros((32, 1), F32)
    for j in range(4):
        mean = mean + jnp.sum(product[32 * j : 32 * j + 32], axis=1, keepdims=True)
    mean = jnp.broadcast_to(mean * (1.0 / LATENT), (32, 128))
    four = lambda v: jnp.concatenate([v] * 4, axis=0)
    grad = (grad - normed[...] * four(mean)) * four(inv[...])
    for k in range(8):
        out[k, :128, :] = grad
        out[k, 128:, :] = rest


def full_table(cos, sin):
    return jnp.concatenate([cos, cos], axis=1), jnp.concatenate([-sin, sin], axis=1)


def part_table(cos, sin):
    one, zero = jnp.ones((cos.shape[0], 64), F32), jnp.zeros((cos.shape[0], 64), F32)
    return jnp.concatenate([cos, cos, one], axis=1), jnp.concatenate([-sin, sin, zero], axis=1)


def seen(seg_row):
    seg_col = jnp.broadcast_to(seg_row, (8, SEQ)).T[:, :1]
    i = lax.broadcasted_iota(jnp.int32, (SEQ, SEQ), 0)
    j = lax.broadcasted_iota(jnp.int32, (SEQ, SEQ), 1)
    return (seg_col == seg_row) & (j <= i)


def softmax(scores, mask):
    scores = jnp.where(mask, scores * (1.0 / math.sqrt(HEAD)), -3e38)
    weights = jnp.exp(scores - jnp.max(scores, axis=1, keepdims=True))
    return weights * (1.0 / jnp.sum(weights, axis=1, keepdims=True))


def lanes(h):
    return pl.ds(pl.multiple_of(h * 128, 128), 128)


def teacher_kernel(
    at, queries, keys, values, cos_full, sin_full, segments, tokens, out, tokens_keep, tokens_send
):
    mask = seen(segments[...])
    cos, sin = full_table(cos_full[...], sin_full[...])
    turn = lambda v: (v * cos + pltpu.roll(v, 64, 1) * sin).astype(BF16)
    key = turn(keys[...].astype(F32))
    value = values[...]

    def pair(p, carry):
        for h in (2 * p, 2 * p + 1):
            query = turn(queries[:, lanes(h)].astype(F32))
            weights = softmax(dot_nt(query, key), mask).astype(BF16)
            out[:, lanes(h)] = dot(weights, value)
        return carry

    lax.fori_loop(0, 4, pair, 0)
    half = lambda c: tokens[:, pl.ds(pl.multiple_of(c * 512, 512), 512)].T
    tokens_keep[...] = half(at[0])
    tokens_send[...] = half(1 - at[0]).astype(F32)


def student_kernel(
    at, packed, queries, key_up, value_up, teacher, cos_part, sin_part, segments,
    grads_keep, grads_send, norm_out, latent, rest, nope, head_values, rest_sum, grads_out,
):
    unpack(packed, latent, rest)
    cos, sin = part_table(cos_part[...], sin_part[...])
    low = low_lanes(SEQ)
    turn = lambda v: v * cos + swap(v) * sin
    rope_key = turn(rest[...])
    nope[...] = dot(latent[...], key_up[...])
    head_values[...] = dot(latent[...], value_up[...]).astype(BF16)
    mask = seen(segments[...])
    scale = 1.0 / math.sqrt(HEAD)
    rest_sum[...] = jnp.zeros_like(rest_sum)

    def head(h, key_part):
        query = turn(queries[:, lanes(h)].astype(F32)).astype(BF16)
        key = jnp.where(low, rope_key, key_part).astype(BF16)
        weights = softmax(dot_nt(query, key), mask)
        weights_low = weights.astype(BF16)
        value = head_values[:, lanes(h)]
        out_grad = (dot(weights_low, value) - teacher[:, lanes(h)]).astype(BF16)
        weight_grad = dot_nt(out_grad, value)
        row = jnp.sum(weights * weight_grad, axis=1, keepdims=True)
        score_grad = (weights * (weight_grad - row) * scale).astype(BF16)
        grads_out[:, lanes(4 + h)] = dot_tn(weights_low, out_grad).astype(BF16)
        return dot_tn(score_grad, query)

    def pair(p, carry):
        both = nope[:, lanes(p)]
        first = head(2 * p, pltpu.roll(both, 64, 1))
        second = head(2 * p + 1, both)
        rest_sum[...] += first + second
        grads_out[:, lanes(p)] = jnp.where(low, pltpu.roll(first, 64, 1), second).astype(BF16)
        return carry

    lax.fori_loop(0, 4, pair, 0)
    wide = dot_nt(grads_out[:, :512], key_up[...]) + dot_nt(grads_out[:, 512:], value_up[...])
    rest_all = rest_sum[...]
    for ref, c in ((grads_keep, at[0]), (grads_send, 1 - at[0])):
        keys = pl.ds(pl.multiple_of(c * 256, 256), 256)
        values = pl.ds(pl.multiple_of(512 + c * 512, 512), 512)
        ref[:, :256] = grads_out[:, keys].astype(ref.dtype)
        ref[:, 256:] = grads_out[:, values].astype(ref.dtype)
    for k in range(8):
        pack(norm_out, k, 32 * k, wide, rest_all)


def up_kernel(at, packed, other_packed, grads, other_grads, *outs):
    *outs, latent, rest = outs
    unpack(packed, latent, rest)
    whole = dot_tn(latent[...], grads[...])
    unpack(other_packed, latent, rest)
    whole = whole + dot_tn(latent[...], other_grads[...].astype(BF16))
    for quarter in range(4):
        for step in range(4):
            @pl.when((at[1] + step) % 4 == quarter)
            def _(quarter=quarter, step=step):
                outs[step][...] = whole[128 * quarter : 128 * quarter + 128]


def split_kernel(at, own, first, second, third, *outs):
    for step in range(4):
        rows = pl.ds(pl.multiple_of((at[2] + step) % 4 * 32, 32), 32)
        outs[step][...] = (own[rows, :] + first[rows, :]) + (second[rows, :] + third[rows, :])


def entry_grad_kernel(at, packed, other_packed, tokens, other_tokens, *refs):
    *outs, grads, other_grads, rest = refs
    for source, ref in ((packed, grads), (other_packed, other_grads)):
        unpack(source, ref, rest)
        ref[:, 512:] = jnp.where(low_lanes(SEQ), rest[...], 0.0).astype(BF16)
    for step in range(4):
        rows = pl.ds(pl.multiple_of((at[1] + step) % 4 * 128, 128), 128)
        whole = dot(tokens[rows, :], grads[...])
        whole = whole + dot(other_tokens[rows, :].astype(BF16), other_grads[...])
        for k in range(4):
            pack(outs[step], k, 32 * k, whole[:, :512], whole[:, 512:])


def entry_split_kernel(at, own, first, second, third, *outs):
    for step in range(4):
        k = (at[2] + step) % 4
        outs[step][...] = (own[k] + first[k]) + (second[k] + third[k])


def entry_sum_kernel(own, first, second, third, out):
    out[...] = (own[...] + first[...]) + (second[...] + third[...])


def up_out_kernel(at, *refs):
    *parts, key_out, value_out = refs
    for c in range(2):
        column = jnp.where(c == 0, at[0], 1 - at[0])
        keys = pl.ds(pl.multiple_of(column * 256, 256), 256)
        values = pl.ds(pl.multiple_of(column * 512, 512), 512)
        for step in range(4):
            ref = parts[4 * c + step]
            for depth in range(4):
                block = (at[1] - step + 4) % 4 * 4 + (at[2] - depth + 4) % 4
                rows = pl.ds(pl.multiple_of(block * 32, 32), 32)
                key_out[rows, keys] = ref[depth, :, :256]
                value_out[rows, values] = ref[depth, :, 256:]


def entry_out_kernel(own, at, *refs):
    parts, (down_out, rope_out, down, rope, rest, sems) = refs[:4], refs[-6:]
    half = at[0] if own else 1 - at[0]
    for step in range(4):
        first = (at[1] - step + 4) % 4
        for depth in range(4):
            spot = (at[2] - depth + 4) % 4 * 32
            rows = pl.ds(pl.multiple_of(first * 128 + spot, 32), 32)
            for j in range(4):
                down[rows, 128 * j : 128 * j + 128] = parts[step][depth, 32 * j : 32 * j + 32, :]
            value = parts[step][depth, 128:PACKED, :]
            rest[pl.ds(pl.multiple_of(spot, 32), 16), :] = value
            rest[pl.ds(pl.multiple_of(spot + 16, 16), 16), :] = pltpu.roll(value, 64, 1)
        rope[:, lanes(first)] = rest[...].T[:64]
    where = pl.ds(pl.multiple_of(half * 512, 512), 512)
    copies = [
        pltpu.make_async_copy(down, down_out.at[where, :], sems.at[0]),
        pltpu.make_async_copy(rope, rope_out.at[:, where], sems.at[1]),
    ]
    for copy in copies:
        copy.start()
    for copy in copies:
        copy.wait()


def stack_kernel(*refs):
    *parts, out = refs
    for k, part in enumerate(parts):
        out[k] = part[...]


def permute(value, move):
    pairs = []
    for i in range(256):
        d, t = divmod(i, 8)
        at = dict(x=d // 8, h=(d // 2) % 4, c=d % 2, y=t // 2, l=t % 2)
        to = {**at, **move(at)}
        j = (to["x"] * 8 + to["h"] * 2 + to["c"]) * 8 + to["y"] * 2 + to["l"]
        pairs.append((i, j))
    return lax.ppermute(value, AXES, pairs)


def other_core(value):
    return permute(value, lambda at: {"c": 1 - at["c"]})


def around(value, axis):
    values = value if isinstance(value, list) else [value] * 3
    moves = [lambda at, k=k: {axis: (at[axis] + k) % 4} for k in (1, 2, 3)]
    return [permute(v, move) for v, move in zip(values, moves)]


def exchange(parts):
    return lax.all_to_all(parts, "tensor", 0, 0, tiled=True)


def tables(segments):
    index = jnp.arange(SEQ, dtype=jnp.int32)
    start = jnp.sum((segments[None, :] < segments[:, None]).astype(jnp.int32), axis=1)
    position = (index - start).astype(F32)

    def angles(width):
        exponent = jnp.arange(width // 2, dtype=F32) * (2.0 / width)
        return position[:, None] * jnp.exp(-exponent * jnp.log(F32(THETA)))[None, :]

    full, part = angles(HEAD), angles(ROPE)
    return (jnp.cos(full), jnp.sin(full)), (jnp.cos(part), jnp.sin(part))


def local(tokens, segment_ids, queries, keys, values, down, rope, key_up, value_up):
    tokens, segments, queries = tokens[0], segment_ids[0], queries[0]
    d = lax.axis_index("dp")
    at = jnp.stack([d % 2, d // 8, d // 2 % 4, lax.axis_index("tensor")])
    seg_row = segments[None, :]
    chunks = shape(8, PACKED, 128)
    unpacked = [pltpu.VMEM((SEQ, LATENT), BF16), pltpu.VMEM((SEQ, 128), F32)]

    (part,) = call(entry_kernel, [chunks], tokens, down, rope, flops=2 * 256 * 1024 * 576, mib=60)
    parts = exchange(part)
    full, partial = tables(segments)
    teacher, tokens_keep, tokens_send = call(
        teacher_kernel,
        [shape(SEQ, 1024), shape(512, SEQ, dtype=BF16), shape(512, SEQ)],
        at, queries, keys[0], values[0], *full, seg_row, tokens,
        scalars=1, flops=4 * 8 * 256 * 256 * 128, mib=60,
    )
    tokens_other = other_core(tokens_send)
    parts, teacher = lax.optimization_barrier((parts, teacher))
    replicas, normed, inv = call(norm_kernel, [chunks, shape(128, 128), shape(32, 128)], parts)
    packed = exchange(replicas)
    packed_other = other_core(packed)
    grads_keep, grads_send, part = call(
        student_kernel,
        [shape(SEQ, 768, dtype=BF16), shape(SEQ, 768), chunks],
        at, packed, queries, key_up, value_up, teacher, *partial, seg_row,
        scalars=1,
        scratch=unpacked + [
            pltpu.VMEM((SEQ, 512), F32),
            pltpu.VMEM((SEQ, 1024), BF16),
            pltpu.VMEM((SEQ, 128), F32),
            pltpu.VMEM((SEQ, 1536), BF16),
        ],
        flops=10 * 8 * 256 * 256 * 128, mib=60,
    )
    grads_other = other_core(grads_send)
    parts = exchange(part)
    quarters = call(
        up_kernel, [shape(128, 768)] * 4, at, packed, packed_other, grads_keep, grads_other,
        scalars=1, scratch=unpacked, flops=2 * 512 * 512 * 768, mib=60,
    )
    received = around(list(quarters[1:]), "x")
    (replicas,) = call(norm_grad_kernel, [chunks], at, parts, normed, inv, *partial, scalars=1)
    packed = exchange(replicas)
    packed_other = other_core(packed)
    quarters = call(split_kernel, [shape(32, 768)] * 4, at, quarters[0], *received, scalars=1)
    received = around(list(quarters[1:]), "h")
    entries = call(
        entry_grad_kernel, [shape(4, PACKED, 128)] * 4,
        at, packed, packed_other, tokens_keep, tokens_other, scalars=1,
        scratch=[pltpu.VMEM((SEQ, 640), BF16)] * 2 + [pltpu.VMEM((SEQ, 128), F32)],
        flops=2 * 512 * 512 * 640,
    )
    arrived = around(list(entries[1:]), "x")
    up = (quarters[0] + received[0]) + (received[1] + received[2])
    (up_all,) = call(stack_kernel, [shape(4, 32, 768)], up, *around(up, "h"))
    entries = call(
        entry_split_kernel, [shape(PACKED, 128)] * 4, at, entries[0], *arrived, scalars=1,
    )
    arrived = around(list(entries[1:]), "h")
    received = [up_all] + around(up_all, "x")
    (entry,) = call(entry_sum_kernel, [shape(PACKED, 128)], entries[0], *arrived)
    entry = jnp.stack([entry] + around(entry, "h"))
    entries = [entry] + around(entry, "x")
    others = [other_core(v) for v in received]
    grad_key, grad_value = call(
        up_out_kernel, [shape(512, 512), shape(512, 1024)], at, *received, *others, scalars=1,
    )
    others = [other_core(v) for v in entries]
    outs = [shape(1024, 512), shape(64, 1024)]
    scratch = [
        pltpu.VMEM((512, 512), F32),
        pltpu.VMEM((64, 512), F32),
        pltpu.VMEM((128, 128), F32),
        pltpu.SemaphoreType.DMA((2,)),
    ]
    halves = call(
        functools.partial(entry_out_kernel, True), outs, at, *entries, scalars=1,
        scratch=scratch, aliases={},
    )
    grad_down, grad_rope = call(
        functools.partial(entry_out_kernel, False), outs, at, *others, *halves, scalars=1,
        scratch=scratch, aliases={5: 0, 6: 1},
    )
    return grad_down, grad_rope, grad_key, grad_value


def solution(mesh):
    token = P("dp", None, "tensor")
    rows, columns = P("tensor", None), P(None, "tensor")
    in_specs = (token, P("dp", None), token, token, token, rows, columns, columns, columns)
    out_specs = (rows, columns, columns, columns)
    return jax.shard_map(local, mesh=mesh, in_specs=in_specs, out_specs=out_specs, check_vma=False)
```

```python
import functools
import math

import jax
import jax.numpy as jnp
from jax import lax
from jax.experimental import pallas as pl
from jax.experimental.pallas import tpu as pltpu
from jax.sharding import PartitionSpec as P


HEAD = 128
ROPE = 64
SEQ = 256
LATENT = 512
THETA = 500000.0
EPS = 1e-06
AXES = ("dp", "tensor")
F32 = jnp.float32
BF16 = jnp.bfloat16

NT = (((1,), (1,)), ((), ()))
TN = (((0,), (0,)), ((), ()))
PACKED = 144


def dot(a, b):
    return jnp.dot(a, b, preferred_element_type=F32)


def dot_nt(a, b):
    return lax.dot_general(a, b, NT, preferred_element_type=F32)


def dot_tn(a, b):
    return lax.dot_general(a, b, TN, preferred_element_type=F32)


def call(body, outs, *args, scalars=0, scratch=(), flops=0, mib=20,
         aliases=None, hbm=(), hbm_out=False):
    spec = pl.BlockSpec(memory_space=pltpu.VMEM)
    smem = pl.BlockSpec(memory_space=pltpu.SMEM)
    anywhere = pl.BlockSpec(memory_space=pltpu.HBM)
    specs = [smem] * scalars + [spec] * (len(args) - scalars)
    for k in (*(aliases or {}), *hbm):
        specs[k] = anywhere
    size = sum(a.size * a.dtype.itemsize for a in args)
    size += sum(math.prod(o.shape) * o.dtype.itemsize for o in outs)
    return pl.pallas_call(
        body,
        out_shape=outs,
        in_specs=specs,
        out_specs=[anywhere if hbm_out else spec] * len(outs),
        scratch_shapes=list(scratch),
        input_output_aliases=aliases or {},
        compiler_params=pltpu.CompilerParams(vmem_limit_bytes=mib << 20),
        cost_estimate=pl.CostEstimate(flops=flops, bytes_accessed=size, transcendentals=0),
    )(*args)


def shape(*dims, dtype=F32):
    return jax.ShapeDtypeStruct(dims, dtype)


def low_lanes(rows):
    return lax.broadcasted_iota(jnp.int32, (rows, 128), 1) < 64


def pack_rest(first, second):
    return jnp.where(low_lanes(16), first, pltpu.roll(second, 64, 1))


def swap(value):
    lane = lax.broadcasted_iota(jnp.int32, value.shape, 1)
    return jnp.where(lane < 32, pltpu.roll(value, 96, 1), pltpu.roll(value, 32, 1))


def pack(out, k, rows, wide, rest):
    for j in range(4):
        out[k, 32 * j : 32 * j + 32, :] = wide[rows : rows + 32, 128 * j : 128 * j + 128]
    out[k, 128:PACKED, :] = pack_rest(rest[rows : rows + 16], rest[rows + 16 : rows + 32])


def unpack_rest(value, out, rows):
    out[rows : rows + 16, :] = value
    out[rows + 16 : rows + 32, :] = pltpu.roll(value, 64, 1)


def unpack(packed, wide, rest):
    for k in range(8):
        for j in range(4):
            wide[32 * k : 32 * k + 32, 128 * j : 128 * j + 128] = packed[
                k, 32 * j : 32 * j + 32, :
            ].astype(wide.dtype)
        unpack_rest(packed[k, 128:PACKED, :], rest, 32 * k)


def start(*pairs):
    copies = [pltpu.make_async_copy(source, target, sem) for source, target, sem in pairs]
    for copy in copies:
        copy.start()
    return copies


def wait(copies):
    for copy in copies:
        copy.wait()


def entry_kernel(tokens_in, down_in, rope_in, out, tokens, down, rope, sems):
    chunks = []
    for k in range(4):
        part = pl.ds(256 * k, 256)
        chunks.append(
            start(
                (tokens_in.at[:, part], tokens.at[:, part], sems.at[k, 0]),
                (down_in.at[part, :], down.at[part, :], sems.at[k, 1]),
                (rope_in.at[:, part], rope.at[:, part], sems.at[k, 2]),
            )
        )
    wide, rest = jnp.zeros((SEQ, LATENT), F32), jnp.zeros((SEQ, 64), F32)
    for k in range(4):
        wait(chunks[k])
        part = pl.ds(256 * k, 256)
        wide = wide + dot(tokens[:, part], down[part, :])
        rest = rest + dot_nt(tokens[:, part], rope[:, part])
    rest = jnp.concatenate([rest, jnp.zeros_like(rest)], axis=1)
    for k in range(8):
        pack(out, k, 32 * k, wide, rest)


def norm_kernel(parts, out, normed_out, inv_out):
    total = jnp.sum(parts[...], axis=0)
    square = jnp.zeros((32, 1), F32)
    for j in range(4):
        tile = total[32 * j : 32 * j + 32]
        square = square + jnp.sum(tile * tile, axis=1, keepdims=True)
    inv = lax.rsqrt(square * (1.0 / LATENT) + EPS)
    inv = jnp.broadcast_to(inv, (32, 128))
    inv_out[...] = inv
    normed = total[:128] * jnp.concatenate([inv] * 4, axis=0)
    normed_out[...] = normed
    for k in range(8):
        out[k, :128, :] = normed
        out[k, 128:, :] = total[128:]


def norm_grad_kernel(at, parts, normed, inv, cos_part, sin_part, out):
    total = jnp.sum(parts[...], axis=0)
    rows = pl.ds(pl.multiple_of(at[3] * 32, 32), 32)
    rest = jnp.concatenate([total[128:], pltpu.roll(total[128:], 64, 1)], axis=0)
    cos, sin = part_table(cos_part[rows, :], sin_part[rows, :])
    rest = rest * cos - swap(rest) * sin
    rest = pack_rest(rest[:16], rest[16:])
    grad = total[:128]
    product = grad * normed[...]
    mean = jnp.zeros((32, 1), F32)
    for j in range(4):
        mean = mean + jnp.sum(product[32 * j : 32 * j + 32], axis=1, keepdims=True)
    mean = jnp.broadcast_to(mean * (1.0 / LATENT), (32, 128))
    four = lambda v: jnp.concatenate([v] * 4, axis=0)
    grad = (grad - normed[...] * four(mean)) * four(inv[...])
    for k in range(8):
        out[k, :128, :] = grad
        out[k, 128:, :] = rest


def full_table(cos, sin):
    return jnp.concatenate([cos, cos], axis=1), jnp.concatenate([-sin, sin], axis=1)


def part_table(cos, sin):
    one, zero = jnp.ones((cos.shape[0], 64), F32), jnp.zeros((cos.shape[0], 64), F32)
    return jnp.concatenate([cos, cos, one], axis=1), jnp.concatenate([-sin, sin, zero], axis=1)


def seen(seg_row):
    seg_col = jnp.broadcast_to(seg_row, (8, SEQ)).T[:, :1]
    i = lax.broadcasted_iota(jnp.int32, (SEQ, SEQ), 0)
    j = lax.broadcasted_iota(jnp.int32, (SEQ, SEQ), 1)
    return (seg_col == seg_row) & (j <= i)


def softmax(scores, mask):
    scores = jnp.where(mask, scores * (1.0 / math.sqrt(HEAD)), -3e38)
    weights = jnp.exp(scores - jnp.max(scores, axis=1, keepdims=True))
    return weights * (1.0 / jnp.sum(weights, axis=1, keepdims=True))


def lanes(h):
    return pl.ds(pl.multiple_of(h * 128, 128), 128)


def teacher_kernel(
    at, queries, keys, values, cos_full, sin_full, segments, tokens, out, tokens_keep, tokens_send
):
    mask = seen(segments[...])
    cos, sin = full_table(cos_full[...], sin_full[...])
    turn = lambda v: (v * cos + pltpu.roll(v, 64, 1) * sin).astype(BF16)
    key = turn(keys[...].astype(F32))
    value = values[...]

    def pair(p, carry):
        for h in (2 * p, 2 * p + 1):
            query = turn(queries[:, lanes(h)].astype(F32))
            weights = softmax(dot_nt(query, key), mask).astype(BF16)
            out[:, lanes(h)] = dot(weights, value)
        return carry

    lax.fori_loop(0, 4, pair, 0)
    half = lambda c: tokens[:, pl.ds(pl.multiple_of(c * 512, 512), 512)].T
    tokens_keep[...] = half(at[0])
    tokens_send[...] = half(1 - at[0]).astype(F32)


def student_kernel(
    at, packed, queries_in, key_up_in, value_up_in, teacher_in, cos_part, sin_part, segments,
    keep_out, send_out, norm_out, latent, rest, nope, head_values, rest_sum, grads,
    queries, key_up, value_up, teacher, keep, send, norm, sems,
):
    (get_keys, get_values, *get_others) = start(
        (key_up_in, key_up, sems.at[0]),
        (value_up_in, value_up, sems.at[1]),
        (queries_in, queries, sems.at[2]),
        (teacher_in, teacher, sems.at[3]),
    )
    unpack(packed, latent, rest)
    cos, sin = part_table(cos_part[...], sin_part[...])
    low = low_lanes(SEQ)
    turn = lambda v: v * cos + swap(v) * sin
    rope_key = turn(rest[...])
    wait([get_keys])
    nope[...] = dot(latent[...], key_up[...])
    wait([get_values])
    head_values[...] = dot(latent[...], value_up[...]).astype(BF16)
    mask = seen(segments[...])
    scale = 1.0 / math.sqrt(HEAD)
    rest_sum[...] = jnp.zeros_like(rest_sum)
    wait(get_others)

    def head(h, key_part):
        query = turn(queries[:, lanes(h)].astype(F32)).astype(BF16)
        key = jnp.where(low, rope_key, key_part).astype(BF16)
        weights = softmax(dot_nt(query, key), mask)
        weights_low = weights.astype(BF16)
        value = head_values[:, lanes(h)]
        out_grad = (dot(weights_low, value) - teacher[:, lanes(h)]).astype(BF16)
        weight_grad = dot_nt(out_grad, value)
        row = jnp.sum(weights * weight_grad, axis=1, keepdims=True)
        score_grad = (weights * (weight_grad - row) * scale).astype(BF16)
        grads[:, lanes(4 + h)] = dot_tn(weights_low, out_grad).astype(BF16)
        return dot_tn(score_grad, query)

    def heads(step, carry):
        for p in (2 * step, 2 * step + 1):
            both = nope[:, lanes(p)]
            first = head(2 * p, pltpu.roll(both, 64, 1))
            second = head(2 * p + 1, both)
            rest_sum[...] += first + second
            grads[:, lanes(p)] = jnp.where(low, pltpu.roll(first, 64, 1), second).astype(BF16)
        return carry

    lax.fori_loop(0, 2, heads, 0)
    for ref, c in ((send, 1 - at[0]), (keep, at[0])):
        keys = pl.ds(pl.multiple_of(c * 256, 256), 256)
        values = pl.ds(pl.multiple_of(512 + c * 512, 512), 512)
        ref[:, :256] = grads[:, keys].astype(ref.dtype)
        ref[:, 256:] = grads[:, values].astype(ref.dtype)
    puts = start((send, send_out, sems.at[4]), (keep, keep_out, sems.at[5]))
    wide = dot_nt(grads[:, :512], key_up[...]) + dot_nt(grads[:, 512:], value_up[...])
    rest_all = rest_sum[...]
    for k in range(8):
        pack(norm, k, 32 * k, wide, rest_all)
    wait(puts + start((norm, norm_out, sems.at[6])))


def up_kernel(at, packed, other_packed, grads, other_grads, *outs):
    *outs, latent, rest = outs
    unpack(packed, latent, rest)
    whole = dot_tn(latent[...], grads[...])
    unpack(other_packed, latent, rest)
    whole = whole + dot_tn(latent[...], other_grads[...].astype(BF16))
    for quarter in range(4):
        for step in range(4):
            @pl.when((at[1] + step) % 4 == quarter)
            def _(quarter=quarter, step=step):
                outs[step][...] = whole[128 * quarter : 128 * quarter + 128]


def split_kernel(at, own, first, second, third, *outs):
    for step in range(4):
        rows = pl.ds(pl.multiple_of((at[2] + step) % 4 * 32, 32), 32)
        outs[step][...] = (own[rows, :] + first[rows, :]) + (second[rows, :] + third[rows, :])


def entry_grad_kernel(at, packed, other_packed, tokens, other_tokens, *refs):
    *outs, grads, other_grads, rest = refs
    for source, ref in ((packed, grads), (other_packed, other_grads)):
        unpack(source, ref, rest)
        ref[:, 512:] = jnp.where(low_lanes(SEQ), rest[...], 0.0).astype(BF16)
    for step in range(4):
        rows = pl.ds(pl.multiple_of((at[1] + step) % 4 * 128, 128), 128)
        whole = dot(tokens[rows, :], grads[...])
        whole = whole + dot(other_tokens[rows, :].astype(BF16), other_grads[...])
        for k in range(4):
            pack(outs[step], k, 32 * k, whole[:, :512], whole[:, 512:])


def entry_split_kernel(at, own, first, second, third, *outs):
    for step in range(4):
        k = (at[2] + step) % 4
        outs[step][...] = (own[k] + first[k]) + (second[k] + third[k])


def entry_sum_kernel(own, first, second, third, out):
    out[...] = (own[...] + first[...]) + (second[...] + third[...])


def up_out_kernel(at, *refs):
    *parts, key_out, value_out = refs
    for c in range(2):
        column = jnp.where(c == 0, at[0], 1 - at[0])
        keys = pl.ds(pl.multiple_of(column * 256, 256), 256)
        values = pl.ds(pl.multiple_of(column * 512, 512), 512)
        for step in range(4):
            ref = parts[4 * c + step]
            for depth in range(4):
                block = (at[1] - step + 4) % 4 * 4 + (at[2] - depth + 4) % 4
                rows = pl.ds(pl.multiple_of(block * 32, 32), 32)
                key_out[rows, keys] = ref[depth, :, :256]
                value_out[rows, values] = ref[depth, :, 256:]


def entry_out_kernel(own, at, *refs):
    parts, (down_out, rope_out, down, rope, rest, sems) = refs[:4], refs[-6:]
    half = at[0] if own else 1 - at[0]
    copies = []
    for step in range(4):
        first = (at[1] - step + 4) % 4
        for depth in range(4):
            spot = (at[2] - depth + 4) % 4 * 32
            rows = pl.ds(pl.multiple_of(first * 128 + spot, 32), 32)
            for j in range(4):
                down[rows, 128 * j : 128 * j + 128] = parts[step][depth, 32 * j : 32 * j + 32, :]
            value = parts[step][depth, 128:PACKED, :]
            rest[pl.ds(pl.multiple_of(spot, 32), 16), :] = value
            rest[pl.ds(pl.multiple_of(spot + 16, 16), 16), :] = pltpu.roll(value, 64, 1)
        rope[:, lanes(first)] = rest[...].T[:64]
        group = pl.ds(pl.multiple_of(first * 128, 128), 128)
        where = pl.ds(pl.multiple_of(half * 512 + first * 128, 128), 128)
        copies += start(
            (down.at[group, :], down_out.at[where, :], sems.at[step, 0]),
            (rope.at[:, group], rope_out.at[:, where], sems.at[step, 1]),
        )
    wait(copies)


def stack_kernel(*refs):
    *parts, out = refs
    for k, part in enumerate(parts):
        out[k] = part[...]


def permute(value, move):
    pairs = []
    for i in range(256):
        d, t = divmod(i, 8)
        at = dict(x=d // 8, h=(d // 2) % 4, c=d % 2, y=t // 2, l=t % 2)
        to = {**at, **move(at)}
        j = (to["x"] * 8 + to["h"] * 2 + to["c"]) * 8 + to["y"] * 2 + to["l"]
        pairs.append((i, j))
    return lax.ppermute(value, AXES, pairs)


def other_core(value):
    return permute(value, lambda at: {"c": 1 - at["c"]})


def around(value, axis):
    values = value if isinstance(value, list) else [value] * 3
    moves = [lambda at, k=k: {axis: (at[axis] + k) % 4} for k in (1, 2, 3)]
    return [permute(v, move) for v, move in zip(values, moves)]


def exchange(parts):
    return lax.all_to_all(parts, "tensor", 0, 0, tiled=True)


def tables(segments):
    index = jnp.arange(SEQ, dtype=jnp.int32)
    start = jnp.sum((segments[None, :] < segments[:, None]).astype(jnp.int32), axis=1)
    position = (index - start).astype(F32)

    def angles(width):
        exponent = jnp.arange(width // 2, dtype=F32) * (2.0 / width)
        return position[:, None] * jnp.exp(-exponent * jnp.log(F32(THETA)))[None, :]

    full, part = angles(HEAD), angles(ROPE)
    return (jnp.cos(full), jnp.sin(full)), (jnp.cos(part), jnp.sin(part))


def local(tokens, segment_ids, queries, keys, values, down, rope, key_up, value_up):
    tokens, segments, queries = tokens[0], segment_ids[0], queries[0]
    d = lax.axis_index("dp")
    at = jnp.stack([d % 2, d // 8, d // 2 % 4, lax.axis_index("tensor")])
    seg_row = segments[None, :]
    chunks = shape(8, PACKED, 128)
    unpacked = [pltpu.VMEM((SEQ, LATENT), BF16), pltpu.VMEM((SEQ, 128), F32)]

    (part,) = call(
        entry_kernel, [chunks], tokens, down, rope, hbm=(0, 1, 2),
        scratch=[
            pltpu.VMEM((SEQ, 1024), BF16),
            pltpu.VMEM((1024, LATENT), BF16),
            pltpu.VMEM((64, 1024), BF16),
            pltpu.SemaphoreType.DMA((4, 3)),
        ],
        flops=2 * 256 * 1024 * 576, mib=60,
    )
    parts = exchange(part)
    full, partial = tables(segments)
    teacher, tokens_keep, tokens_send = call(
        teacher_kernel,
        [shape(SEQ, 1024), shape(512, SEQ, dtype=BF16), shape(512, SEQ)],
        at, queries, keys[0], values[0], *full, seg_row, tokens,
        scalars=1, flops=4 * 8 * 256 * 256 * 128, mib=60,
    )
    tokens_other = other_core(tokens_send)
    parts, teacher = lax.optimization_barrier((parts, teacher))
    replicas, normed, inv = call(norm_kernel, [chunks, shape(128, 128), shape(32, 128)], parts)
    packed = exchange(replicas)
    packed_other = other_core(packed)
    grads_keep, grads_send, part = call(
        student_kernel,
        [shape(SEQ, 768, dtype=BF16), shape(SEQ, 768), chunks],
        at, packed, queries, key_up, value_up, teacher, *partial, seg_row,
        scalars=1,
        scratch=unpacked + [
            pltpu.VMEM((SEQ, 512), F32),
            pltpu.VMEM((SEQ, 1024), BF16),
            pltpu.VMEM((SEQ, 128), F32),
            pltpu.VMEM((SEQ, 1536), BF16),
            pltpu.VMEM((SEQ, 1024), BF16),
            pltpu.VMEM((LATENT, 512), BF16),
            pltpu.VMEM((LATENT, 1024), BF16),
            pltpu.VMEM((SEQ, 1024), F32),
            pltpu.VMEM((SEQ, 768), BF16),
            pltpu.VMEM((SEQ, 768), F32),
            pltpu.VMEM((8, PACKED, 128), F32),
            pltpu.SemaphoreType.DMA((7,)),
        ],
        hbm=(2, 3, 4, 5), hbm_out=True,
        flops=10 * 8 * 256 * 256 * 128, mib=60,
    )
    grads_other = other_core(grads_send)
    parts = exchange(part)
    quarters = call(
        up_kernel, [shape(128, 768)] * 4, at, packed, packed_other, grads_keep, grads_other,
        scalars=1, scratch=unpacked, flops=2 * 512 * 512 * 768, mib=60,
    )
    received = around(list(quarters[1:]), "x")
    (replicas,) = call(norm_grad_kernel, [chunks], at, parts, normed, inv, *partial, scalars=1)
    packed = exchange(replicas)
    packed_other = other_core(packed)
    quarters = call(split_kernel, [shape(32, 768)] * 4, at, quarters[0], *received, scalars=1)
    received = around(list(quarters[1:]), "h")
    entries = call(
        entry_grad_kernel, [shape(4, PACKED, 128)] * 4,
        at, packed, packed_other, tokens_keep, tokens_other, scalars=1,
        scratch=[pltpu.VMEM((SEQ, 640), BF16)] * 2 + [pltpu.VMEM((SEQ, 128), F32)],
        flops=2 * 512 * 512 * 640,
    )
    arrived = around(list(entries[1:]), "x")
    up = (quarters[0] + received[0]) + (received[1] + received[2])
    (up_all,) = call(stack_kernel, [shape(4, 32, 768)], up, *around(up, "h"))
    entries = call(
        entry_split_kernel, [shape(PACKED, 128)] * 4, at, entries[0], *arrived, scalars=1,
    )
    arrived = around(list(entries[1:]), "h")
    received = [up_all] + around(up_all, "x")
    (entry,) = call(entry_sum_kernel, [shape(PACKED, 128)], entries[0], *arrived)
    entry = jnp.stack([entry] + around(entry, "h"))
    entries = [entry] + around(entry, "x")
    others = [other_core(v) for v in received]
    grad_key, grad_value = call(
        up_out_kernel, [shape(512, 512), shape(512, 1024)], at, *received, *others, scalars=1,
    )
    others = [other_core(v) for v in entries]
    outs = [shape(1024, 512), shape(64, 1024)]
    scratch = [
        pltpu.VMEM((512, 512), F32),
        pltpu.VMEM((64, 512), F32),
        pltpu.VMEM((128, 128), F32),
        pltpu.SemaphoreType.DMA((4, 2)),
    ]
    halves = call(
        functools.partial(entry_out_kernel, True), outs, at, *entries, scalars=1,
        scratch=scratch, hbm_out=True,
    )
    grad_down, grad_rope = call(
        functools.partial(entry_out_kernel, False), outs, at, *others, *halves, scalars=1,
        scratch=scratch, hbm_out=True, aliases={5: 0, 6: 1},
    )
    return grad_down, grad_rope, grad_key, grad_value


def solution(mesh):
    token = P("dp", None, "tensor")
    rows, columns = P("tensor", None), P(None, "tensor")
    in_specs = (token, P("dp", None), token, token, token, rows, columns, columns, columns)
    out_specs = (rows, columns, columns, columns)
    return jax.shard_map(local, mesh=mesh, in_specs=in_specs, out_specs=out_specs, check_vma=False)
```

```python
import functools
import math

import jax
import jax.numpy as jnp
from jax import lax
from jax.experimental import pallas as pl
from jax.experimental.pallas import tpu as pltpu
from jax.sharding import PartitionSpec as P


HEAD = 128
ROPE = 64
SEQ = 256
LATENT = 512
THETA = 500000.0
EPS = 1e-06
AXES = ("dp", "tensor")
F32 = jnp.float32
BF16 = jnp.bfloat16

NT = (((1,), (1,)), ((), ()))
TN = (((0,), (0,)), ((), ()))
PACKED = 144


def dot(a, b):
    return jnp.dot(a, b, preferred_element_type=F32)


def dot_nt(a, b):
    return lax.dot_general(a, b, NT, preferred_element_type=F32)


def dot_tn(a, b):
    return lax.dot_general(a, b, TN, preferred_element_type=F32)


def call(body, outs, *args, scalars=0, scratch=(), flops=0, mib=20,
         aliases=None, hbm=(), hbm_out=False):
    spec = pl.BlockSpec(memory_space=pltpu.VMEM)
    smem = pl.BlockSpec(memory_space=pltpu.SMEM)
    anywhere = pl.BlockSpec(memory_space=pltpu.HBM)
    specs = [smem] * scalars + [spec] * (len(args) - scalars)
    for k in (*(aliases or {}), *hbm):
        specs[k] = anywhere
    size = sum(a.size * a.dtype.itemsize for a in args)
    size += sum(math.prod(o.shape) * o.dtype.itemsize for o in outs)
    return pl.pallas_call(
        body,
        out_shape=outs,
        in_specs=specs,
        out_specs=[anywhere if hbm_out else spec] * len(outs),
        scratch_shapes=list(scratch),
        input_output_aliases=aliases or {},
        compiler_params=pltpu.CompilerParams(vmem_limit_bytes=mib << 20),
        cost_estimate=pl.CostEstimate(flops=flops, bytes_accessed=size, transcendentals=0),
    )(*args)


def shape(*dims, dtype=F32):
    return jax.ShapeDtypeStruct(dims, dtype)


def low_lanes(rows):
    return lax.broadcasted_iota(jnp.int32, (rows, 128), 1) < 64


def pack_rest(first, second):
    return jnp.where(low_lanes(16), first, pltpu.roll(second, 64, 1))


def swap(value):
    lane = lax.broadcasted_iota(jnp.int32, value.shape, 1)
    return jnp.where(lane < 32, pltpu.roll(value, 96, 1), pltpu.roll(value, 32, 1))


def pack(out, k, rows, wide, rest):
    for j in range(4):
        out[k, 32 * j : 32 * j + 32, :] = wide[rows : rows + 32, 128 * j : 128 * j + 128]
    out[k, 128:PACKED, :] = pack_rest(rest[rows : rows + 16], rest[rows + 16 : rows + 32])


def unpack_rest(value, out, rows):
    out[rows : rows + 16, :] = value
    out[rows + 16 : rows + 32, :] = pltpu.roll(value, 64, 1)


def unpack(packed, wide, rest):
    for k in range(8):
        for j in range(4):
            wide[32 * k : 32 * k + 32, 128 * j : 128 * j + 128] = packed[
                k, 32 * j : 32 * j + 32, :
            ].astype(wide.dtype)
        unpack_rest(packed[k, 128:PACKED, :], rest, 32 * k)


def start(*pairs):
    copies = [pltpu.make_async_copy(source, target, sem) for source, target, sem in pairs]
    for copy in copies:
        copy.start()
    return copies


def wait(copies):
    for copy in copies:
        copy.wait()


def start(*pairs):
    copies = [pltpu.make_async_copy(source, target, sem) for source, target, sem in pairs]
    for copy in copies:
        copy.start()
    return copies


def wait(copies):
    for copy in copies:
        copy.wait()


def entry_kernel(tokens, down, rope, out):
    wide = dot(tokens[...], down[...])
    rest = dot_nt(tokens[...], rope[...])
    rest = jnp.concatenate([rest, jnp.zeros_like(rest)], axis=1)
    for k in range(8):
        pack(out, k, 32 * k, wide, rest)


def norm_kernel(parts, out, normed_out, inv_out):
    total = jnp.sum(parts[...], axis=0)
    square = jnp.zeros((32, 1), F32)
    for j in range(4):
        tile = total[32 * j : 32 * j + 32]
        square = square + jnp.sum(tile * tile, axis=1, keepdims=True)
    inv = lax.rsqrt(square * (1.0 / LATENT) + EPS)
    inv = jnp.broadcast_to(inv, (32, 128))
    inv_out[...] = inv
    normed = total[:128] * jnp.concatenate([inv] * 4, axis=0)
    normed_out[...] = normed
    for k in range(8):
        out[k, :128, :] = normed
        out[k, 128:, :] = total[128:]


def norm_grad_kernel(at, parts, normed, inv, cos_part, sin_part, out):
    total = jnp.sum(parts[...], axis=0)
    rows = pl.ds(pl.multiple_of(at[3] * 32, 32), 32)
    rest = jnp.concatenate([total[128:], pltpu.roll(total[128:], 64, 1)], axis=0)
    cos, sin = part_table(cos_part[rows, :], sin_part[rows, :])
    rest = rest * cos - swap(rest) * sin
    rest = pack_rest(rest[:16], rest[16:])
    grad = total[:128]
    product = grad * normed[...]
    mean = jnp.zeros((32, 1), F32)
    for j in range(4):
        mean = mean + jnp.sum(product[32 * j : 32 * j + 32], axis=1, keepdims=True)
    mean = jnp.broadcast_to(mean * (1.0 / LATENT), (32, 128))
    four = lambda v: jnp.concatenate([v] * 4, axis=0)
    grad = (grad - normed[...] * four(mean)) * four(inv[...])
    for k in range(8):
        out[k, :128, :] = grad
        out[k, 128:, :] = rest


def full_table(cos, sin):
    return jnp.concatenate([cos, cos], axis=1), jnp.concatenate([-sin, sin], axis=1)


def part_table(cos, sin):
    one, zero = jnp.ones((cos.shape[0], 64), F32), jnp.zeros((cos.shape[0], 64), F32)
    return jnp.concatenate([cos, cos, one], axis=1), jnp.concatenate([-sin, sin, zero], axis=1)


def seen(seg_row):
    seg_col = jnp.broadcast_to(seg_row, (8, SEQ)).T[:, :1]
    i = lax.broadcasted_iota(jnp.int32, (SEQ, SEQ), 0)
    j = lax.broadcasted_iota(jnp.int32, (SEQ, SEQ), 1)
    return (seg_col == seg_row) & (j <= i)


def softmax(scores, mask):
    scores = jnp.where(mask, scores * (1.0 / math.sqrt(HEAD)), -3e38)
    weights = jnp.exp(scores - jnp.max(scores, axis=1, keepdims=True))
    return weights * (1.0 / jnp.sum(weights, axis=1, keepdims=True))


def lanes(h):
    return pl.ds(pl.multiple_of(h * 128, 128), 128)


def teacher_kernel(
    at, queries, keys, values, cos_full, sin_full, segments, tokens, out, tokens_keep, tokens_send
):
    mask = seen(segments[...])
    cos, sin = full_table(cos_full[...], sin_full[...])
    turn = lambda v: (v * cos + pltpu.roll(v, 64, 1) * sin).astype(BF16)
    key = turn(keys[...].astype(F32))
    value = values[...]

    def pair(p, carry):
        for h in (2 * p, 2 * p + 1):
            query = turn(queries[:, lanes(h)].astype(F32))
            weights = softmax(dot_nt(query, key), mask).astype(BF16)
            out[:, lanes(h)] = dot(weights, value)
        return carry

    lax.fori_loop(0, 4, pair, 0)
    half = lambda c: tokens[:, pl.ds(pl.multiple_of(c * 512, 512), 512)].T
    tokens_keep[...] = half(at[0])
    tokens_send[...] = half(1 - at[0]).astype(F32)


def student_kernel(
    at, packed_in, queries_in, key_up_in, value_up_in, teacher_in, cos_part, sin_part, segments,
    keep_out, send_out, norm_out, latent, rest, nope, head_values, rest_sum, grads,
    packed, queries, key_up, value_up, teacher, keep, send, norm, sems,
):
    (get_packed, get_keys, get_values, *get_others) = start(
        (packed_in, packed, sems.at[8]),
        (key_up_in, key_up, sems.at[0]),
        (value_up_in, value_up, sems.at[1]),
        (queries_in, queries, sems.at[2]),
        (teacher_in, teacher, sems.at[3]),
    )
    wait([get_packed])
    unpack(packed, latent, rest)
    cos, sin = part_table(cos_part[...], sin_part[...])
    low = low_lanes(SEQ)
    turn = lambda v: v * cos + swap(v) * sin
    rope_key = turn(rest[...])
    wait([get_keys])
    nope[...] = dot(latent[...], key_up[...])
    wait([get_values])
    head_values[...] = dot(latent[...], value_up[...]).astype(BF16)
    mask = seen(segments[...])
    scale = 1.0 / math.sqrt(HEAD)
    rest_sum[...] = jnp.zeros_like(rest_sum)
    wait(get_others)

    def head(h, key_part):
        query = turn(queries[:, lanes(h)].astype(F32)).astype(BF16)
        key = jnp.where(low, rope_key, key_part).astype(BF16)
        weights = softmax(dot_nt(query, key), mask)
        weights_low = weights.astype(BF16)
        value = head_values[:, lanes(h)]
        out_grad = (dot(weights_low, value) - teacher[:, lanes(h)]).astype(BF16)
        weight_grad = dot_nt(out_grad, value)
        row = jnp.sum(weights * weight_grad, axis=1, keepdims=True)
        score_grad = (weights * (weight_grad - row) * scale).astype(BF16)
        grads[:, lanes(4 + h)] = dot_tn(weights_low, out_grad).astype(BF16)
        return dot_tn(score_grad, query)

    def heads(step, carry):
        for p in (2 * step, 2 * step + 1):
            both = nope[:, lanes(p)]
            first = head(2 * p, pltpu.roll(both, 64, 1))
            second = head(2 * p + 1, both)
            rest_sum[...] += first + second
            grads[:, lanes(p)] = jnp.where(low, pltpu.roll(first, 64, 1), second).astype(BF16)
        return carry

    lax.fori_loop(0, 2, heads, 0)
    for ref, c in ((send, 1 - at[0]), (keep, at[0])):
        keys = pl.ds(pl.multiple_of(c * 256, 256), 256)
        values = pl.ds(pl.multiple_of(512 + c * 512, 512), 512)
        ref[:, :256] = grads[:, keys].astype(ref.dtype)
        ref[:, 256:] = grads[:, values].astype(ref.dtype)
    puts = start((send, send_out, sems.at[4]), (keep, keep_out, sems.at[5]))
    for r in range(2):
        rows = slice(128 * r, 128 * r + 128)
        wide = dot_nt(grads[rows, :512], key_up[...]) + dot_nt(grads[rows, 512:], value_up[...])
        rest_half = rest_sum[rows]
        for k in range(4):
            pack(norm, 4 * r + k, 32 * k, wide, rest_half)
        part = pl.ds(4 * r, 4)
        puts += start((norm.at[part], norm_out.at[part], sems.at[6 + r]))
    wait(puts)


def up_kernel(at, packed_in, other_packed_in, grads_in, other_grads_in, *refs):
    *outs, latent, rest, packed, other_packed, grads, other_grads, whole, sems = refs
    gets = start(
        (packed_in, packed, sems.at[0]),
        (grads_in, grads, sems.at[1]),
        (other_packed_in, other_packed, sems.at[2]),
        (other_grads_in, other_grads, sems.at[3]),
    )
    wait(gets[:1])
    unpack(packed, latent, rest)
    wait(gets[1:2])
    whole[...] = dot_tn(latent[...], grads[...])
    wait(gets[2:3])
    unpack(other_packed, latent, rest)
    wait(gets[3:])
    whole[...] += dot_tn(latent[...], other_grads[...].astype(BF16))
    puts = []
    for step in range(4):
        rows = pl.ds(pl.multiple_of((at[1] + step) % 4 * 128, 128), 128)
        puts += start((whole.at[rows, :], outs[step], sems.at[step]))
    wait(puts)


def halves_kernel(own, first, second, third, *outs):
    n = outs[0].shape[0]
    for k, out in enumerate(outs):
        rows = slice(n * k, n * k + n)
        out[...] = (own[rows] + first[rows]) + (second[rows] + third[rows])


def add_kernel(a, b, got_a, got_b, a_out, b_out):
    a_out[...] = a[...] + got_a[...]
    b_out[...] = b[...] + got_b[...]


def add_stack_kernel(a, b, got_a, got_b, out):
    n = a.shape[0]
    out[:n] = a[...] + got_a[...]
    out[n:] = b[...] + got_b[...]


def entry_grad_kernel(at, packed, other_packed, tokens, other_tokens, *refs):
    *outs, grads, other_grads, rest = refs
    for source, ref in ((packed, grads), (other_packed, other_grads)):
        unpack(source, ref, rest)
        ref[:, 512:] = jnp.where(low_lanes(SEQ), rest[...], 0.0).astype(BF16)
    for step in range(4):
        rows = pl.ds(pl.multiple_of((at[1] + step) % 4 * 128, 128), 128)
        whole = dot(tokens[rows, :], grads[...])
        whole = whole + dot(other_tokens[rows, :].astype(BF16), other_grads[...])
        for k in range(4):
            pack(outs[step], k, 32 * k, whole[:, :512], whole[:, 512:])


def up_out_kernel(at, *refs):
    *parts, key_out, value_out = refs
    for c in range(2):
        column = jnp.where(c == 0, at[0], 1 - at[0])
        keys = pl.ds(pl.multiple_of(column * 256, 256), 256)
        values = pl.ds(pl.multiple_of(column * 512, 512), 512)
        for step in range(4):
            ref = parts[4 * c + step]
            rows = pl.ds(pl.multiple_of((at[1] - step + 4) % 4 * 128, 128), 128)
            key_out[rows, keys] = ref[:, :256]
            value_out[rows, values] = ref[:, 256:]


def entry_out_kernel(blocks, at, *refs):
    parts, (down_out, rope_out, down, rope, rest, sems) = refs[: len(blocks)], refs[-6:]
    copies = []
    for b, (own, step) in enumerate(blocks):
        half = at[0] if own else 1 - at[0]
        for depth in range(4):
            for j in range(4):
                down[b, 32 * depth : 32 * depth + 32, 128 * j : 128 * j + 128] = parts[b][
                    depth, 32 * j : 32 * j + 32, :
                ]
            unpack_rest(parts[b][depth, 128:PACKED, :], rest, 32 * depth)
        rope[b] = rest[...].T[:64]
        first = half * 512 + (at[1] - step + 4) % 4 * 128
        where = pl.ds(pl.multiple_of(first, 128), 128)
        copies += start(
            (down.at[b], down_out.at[where, :], sems.at[b, 0]),
            (rope.at[b], rope_out.at[:, where], sems.at[b, 1]),
        )
    wait(copies)


def permute(value, move):
    pairs = []
    for i in range(256):
        d, t = divmod(i, 8)
        at = dict(x=d // 8, h=(d // 2) % 4, c=d % 2, y=t // 2, l=t % 2)
        to = {**at, **move(at)}
        j = (to["x"] * 8 + to["h"] * 2 + to["c"]) * 8 + to["y"] * 2 + to["l"]
        pairs.append((i, j))
    return lax.ppermute(value, AXES, pairs)


def other_core(value):
    return permute(value, lambda at: {"c": 1 - at["c"]})


def around(value, axis):
    values = value if isinstance(value, list) else [value] * 3
    out = []
    for k in (1, 2, 3):
        out.append(permute(values[k - 1], lambda at: {axis: (at[axis] + k) % 4}))
    return out


def partners(a, b, masks):
    return [permute(v, lambda at, m=m: {"h": at["h"] ^ m}) for v, m in zip((a, b), masks)]


def exchange(parts):
    return lax.all_to_all(parts, "tensor", 0, 0, tiled=True)


def tables(segments):
    index = jnp.arange(SEQ, dtype=jnp.int32)
    start = jnp.sum((segments[None, :] < segments[:, None]).astype(jnp.int32), axis=1)
    position = (index - start).astype(F32)

    def angles(width):
        exponent = jnp.arange(width // 2, dtype=F32) * (2.0 / width)
        return position[:, None] * jnp.exp(-exponent * jnp.log(F32(THETA)))[None, :]

    full, part = angles(HEAD), angles(ROPE)
    return (jnp.cos(full), jnp.sin(full)), (jnp.cos(part), jnp.sin(part))


def local(tokens, segment_ids, queries, keys, values, down, rope, key_up, value_up):
    tokens, segments, queries = tokens[0], segment_ids[0], queries[0]
    d = lax.axis_index("dp")
    at = jnp.stack([d % 2, d // 8, d // 2 % 4, lax.axis_index("tensor")])
    seg_row = segments[None, :]
    chunks = shape(8, PACKED, 128)
    unpacked = [pltpu.VMEM((SEQ, LATENT), BF16), pltpu.VMEM((SEQ, 128), F32)]

    (part,) = call(entry_kernel, [chunks], tokens, down, rope, flops=2 * 256 * 1024 * 576, mib=60)
    parts = exchange(part)
    full, partial = tables(segments)
    teacher, tokens_keep, tokens_send = call(
        teacher_kernel,
        [shape(SEQ, 1024), shape(512, SEQ, dtype=BF16), shape(512, SEQ)],
        at, queries, keys[0], values[0], *full, seg_row, tokens,
        scalars=1, flops=4 * 8 * 256 * 256 * 128, mib=60,
    )
    tokens_other = other_core(tokens_send)
    parts, teacher = lax.optimization_barrier((parts, teacher))
    replicas, normed, inv = call(norm_kernel, [chunks, shape(128, 128), shape(32, 128)], parts)
    packed = exchange(replicas)
    packed_other = other_core(packed)
    grads_keep, grads_send, part = call(
        student_kernel,
        [shape(SEQ, 768, dtype=BF16), shape(SEQ, 768), chunks],
        at, packed, queries, key_up, value_up, teacher, *partial, seg_row,
        scalars=1,
        scratch=unpacked + [
            pltpu.VMEM((SEQ, 512), F32),
            pltpu.VMEM((SEQ, 1024), BF16),
            pltpu.VMEM((SEQ, 128), F32),
            pltpu.VMEM((SEQ, 1536), BF16),
            pltpu.VMEM((8, PACKED, 128), F32),
            pltpu.VMEM((SEQ, 1024), BF16),
            pltpu.VMEM((LATENT, 512), BF16),
            pltpu.VMEM((LATENT, 1024), BF16),
            pltpu.VMEM((SEQ, 1024), F32),
            pltpu.VMEM((SEQ, 768), BF16),
            pltpu.VMEM((SEQ, 768), F32),
            pltpu.VMEM((8, PACKED, 128), F32),
            pltpu.SemaphoreType.DMA((9,)),
        ],
        hbm=(1, 2, 3, 4, 5), hbm_out=True,
        flops=10 * 8 * 256 * 256 * 128, mib=60,
    )
    grads_other = other_core(grads_send)
    parts = exchange(part)
    quarters = call(
        up_kernel, [shape(128, 768)] * 4, at, packed, packed_other, grads_keep, grads_other,
        scalars=1, hbm=(1, 2, 3, 4), hbm_out=True,
        scratch=unpacked + [
            pltpu.VMEM((8, PACKED, 128), F32),
            pltpu.VMEM((8, PACKED, 128), F32),
            pltpu.VMEM((SEQ, 768), BF16),
            pltpu.VMEM((SEQ, 768), F32),
            pltpu.VMEM((LATENT, 768), F32),
            pltpu.SemaphoreType.DMA((4,)),
        ],
        flops=2 * 512 * 512 * 768, mib=60,
    )
    received = around(list(quarters[1:]), "x")
    (replicas,) = call(norm_grad_kernel, [chunks], at, parts, normed, inv, *partial, scalars=1)
    packed = exchange(replicas)
    packed_other = other_core(packed)
    halves = call(halves_kernel, [shape(64, 768)] * 2, quarters[0], *received)
    received = partners(*halves, (1, 3))
    entries = call(
        entry_grad_kernel, [shape(4, PACKED, 128)] * 4,
        at, packed, packed_other, tokens_keep, tokens_other, scalars=1,
        scratch=[pltpu.VMEM((SEQ, 640), BF16)] * 2 + [pltpu.VMEM((SEQ, 128), F32)],
        flops=2 * 512 * 512 * 640,
    )
    arrived = around(list(entries[1:]), "x")
    halves = call(add_kernel, [shape(64, 768)] * 2, *halves, *received)
    received = partners(*halves, (3, 1))
    entry = call(halves_kernel, [shape(2, PACKED, 128)] * 2, entries[0], *arrived)
    arrived = partners(*entry, (1, 3))
    (up,) = call(add_stack_kernel, [shape(128, 768)], *halves, *received)
    received = [up] + around(up, "x")
    entry = call(add_kernel, [shape(2, PACKED, 128)] * 2, *entry, *arrived)
    arrived = partners(*entry, (3, 1))
    (entry,) = call(add_stack_kernel, [shape(4, PACKED, 128)], *entry, *arrived)
    entries = [entry] + around(entry, "x")
    others = [other_core(v) for v in received]
    grad_key, grad_value = call(
        up_out_kernel, [shape(512, 512), shape(512, 1024)], at, *received, *others, scalars=1,
    )
    others = [other_core(v) for v in entries]
    done = []
    for blocks in (
        ((True, 0), (True, 1), (True, 2), (False, 0), (False, 1)),
        ((True, 3), (False, 2)),
        ((False, 3),),
    ):
        count = len(blocks)
        done = call(
            functools.partial(entry_out_kernel, blocks),
            [shape(1024, 512), shape(64, 1024)],
            at, *[(entries if own else others)[k] for own, k in blocks], *done, scalars=1,
            scratch=[
                pltpu.VMEM((count, 128, 512), F32),
                pltpu.VMEM((count, 64, 128), F32),
                pltpu.VMEM((128, 128), F32),
                pltpu.SemaphoreType.DMA((count, 2)),
            ],
            hbm_out=True, aliases={count + 1: 0, count + 2: 1} if done else None,
        )
    grad_down, grad_rope = done
    return grad_down, grad_rope, grad_key, grad_value


def solution(mesh):
    token = P("dp", None, "tensor")
    rows, columns = P("tensor", None), P(None, "tensor")
    in_specs = (token, P("dp", None), token, token, token, rows, columns, columns, columns)
    out_specs = (rows, columns, columns, columns)
    return jax.shard_map(local, mesh=mesh, in_specs=in_specs, out_specs=out_specs, check_vma=False)
```

```python
import functools
import math

import jax
import jax.numpy as jnp
from jax import lax
from jax.experimental import pallas as pl
from jax.experimental.pallas import tpu as pltpu
from jax.sharding import PartitionSpec as P


HEAD = 128
ROPE = 64
SEQ = 256
LATENT = 512
THETA = 500000.0
EPS = 1e-06
AXES = ("dp", "tensor")
F32 = jnp.float32
BF16 = jnp.bfloat16

NT = (((1,), (1,)), ((), ()))
TN = (((0,), (0,)), ((), ()))
PACKED = 144


def dot(a, b):
    return jnp.dot(a, b, preferred_element_type=F32)


def dot_nt(a, b):
    return lax.dot_general(a, b, NT, preferred_element_type=F32)


def dot_tn(a, b):
    return lax.dot_general(a, b, TN, preferred_element_type=F32)


def call(body, outs, *args, scalars=0, scratch=(), flops=0, mib=20,
         aliases=None, hbm=(), hbm_out=False):
    spec = pl.BlockSpec(memory_space=pltpu.VMEM)
    smem = pl.BlockSpec(memory_space=pltpu.SMEM)
    anywhere = pl.BlockSpec(memory_space=pltpu.HBM)
    specs = [smem] * scalars + [spec] * (len(args) - scalars)
    for k in (*(aliases or {}), *hbm):
        specs[k] = anywhere
    size = sum(a.size * a.dtype.itemsize for a in args)
    size += sum(math.prod(o.shape) * o.dtype.itemsize for o in outs)
    return pl.pallas_call(
        body,
        out_shape=outs,
        in_specs=specs,
        out_specs=[anywhere if hbm_out else spec] * len(outs),
        scratch_shapes=list(scratch),
        input_output_aliases=aliases or {},
        compiler_params=pltpu.CompilerParams(vmem_limit_bytes=mib << 20),
        cost_estimate=pl.CostEstimate(flops=flops, bytes_accessed=size, transcendentals=0),
    )(*args)


def shape(*dims, dtype=F32):
    return jax.ShapeDtypeStruct(dims, dtype)


def low_lanes(rows):
    return lax.broadcasted_iota(jnp.int32, (rows, 128), 1) < 64


def pack_rest(first, second):
    return jnp.where(low_lanes(16), first, pltpu.roll(second, 64, 1))


def swap(value):
    lane = lax.broadcasted_iota(jnp.int32, value.shape, 1)
    return jnp.where(lane < 32, pltpu.roll(value, 96, 1), pltpu.roll(value, 32, 1))


def pack(out, k, rows, wide, rest):
    for j in range(4):
        out[k, 32 * j : 32 * j + 32, :] = wide[rows : rows + 32, 128 * j : 128 * j + 128]
    out[k, 128:PACKED, :] = pack_rest(rest[rows : rows + 16], rest[rows + 16 : rows + 32])


def unpack_rest(value, out, rows):
    out[rows : rows + 16, :] = value
    out[rows + 16 : rows + 32, :] = pltpu.roll(value, 64, 1)


def unpack(packed, wide, rest):
    for k in range(8):
        for j in range(4):
            wide[32 * k : 32 * k + 32, 128 * j : 128 * j + 128] = packed[
                k, 32 * j : 32 * j + 32, :
            ].astype(wide.dtype)
        unpack_rest(packed[k, 128:PACKED, :], rest, 32 * k)


def start(*pairs):
    copies = [pltpu.make_async_copy(source, target, sem) for source, target, sem in pairs]
    for copy in copies:
        copy.start()
    return copies


def wait(copies):
    for copy in copies:
        copy.wait()


def entry_kernel(tokens, down, rope, out):
    wide = dot(tokens[...], down[...])
    rest = dot_nt(tokens[...], rope[...])
    rest = jnp.concatenate([rest, jnp.zeros_like(rest)], axis=1)
    for k in range(8):
        pack(out, k, 32 * k, wide, rest)


def norm_kernel(parts, out, normed_out, inv_out):
    total = jnp.sum(parts[...], axis=0)
    square = jnp.zeros((32, 1), F32)
    for j in range(4):
        tile = total[32 * j : 32 * j + 32]
        square = square + jnp.sum(tile * tile, axis=1, keepdims=True)
    inv = lax.rsqrt(square * (1.0 / LATENT) + EPS)
    inv = jnp.broadcast_to(inv, (32, 128))
    inv_out[...] = inv
    normed = total[:128] * jnp.concatenate([inv] * 4, axis=0)
    normed_out[...] = normed
    for k in range(8):
        out[k, :128, :] = normed
        out[k, 128:, :] = total[128:]


def norm_grad_kernel(at, parts, normed, inv, cos_part, sin_part, out):
    total = jnp.sum(parts[...], axis=0)
    rows = pl.ds(pl.multiple_of(at[3] * 32, 32), 32)
    rest = jnp.concatenate([total[128:], pltpu.roll(total[128:], 64, 1)], axis=0)
    cos, sin = part_table(cos_part[rows, :], sin_part[rows, :])
    rest = rest * cos - swap(rest) * sin
    rest = pack_rest(rest[:16], rest[16:])
    grad = total[:128]
    product = grad * normed[...]
    mean = jnp.zeros((32, 1), F32)
    for j in range(4):
        mean = mean + jnp.sum(product[32 * j : 32 * j + 32], axis=1, keepdims=True)
    mean = jnp.broadcast_to(mean * (1.0 / LATENT), (32, 128))
    four = lambda v: jnp.concatenate([v] * 4, axis=0)
    grad = (grad - normed[...] * four(mean)) * four(inv[...])
    for k in range(8):
        out[k, :128, :] = grad
        out[k, 128:, :] = rest


def full_table(cos, sin):
    return jnp.concatenate([cos, cos], axis=1), jnp.concatenate([-sin, sin], axis=1)


def part_table(cos, sin):
    one, zero = jnp.ones((cos.shape[0], 64), F32), jnp.zeros((cos.shape[0], 64), F32)
    return jnp.concatenate([cos, cos, one], axis=1), jnp.concatenate([-sin, sin, zero], axis=1)


def seen(seg_row):
    seg_col = jnp.broadcast_to(seg_row, (8, SEQ)).T[:, :1]
    i = lax.broadcasted_iota(jnp.int32, (SEQ, SEQ), 0)
    j = lax.broadcasted_iota(jnp.int32, (SEQ, SEQ), 1)
    return (seg_col == seg_row) & (j <= i)


def softmax(scores, mask):
    scores = jnp.where(mask, scores * (1.0 / math.sqrt(HEAD)), -3e38)
    weights = jnp.exp(scores - jnp.max(scores, axis=1, keepdims=True))
    return weights * (1.0 / jnp.sum(weights, axis=1, keepdims=True))


def lanes(h):
    return pl.ds(pl.multiple_of(h * 128, 128), 128)


def teacher_kernel(
    at, queries, keys, values, cos_full, sin_full, segments, tokens, out, tokens_keep, tokens_send
):
    mask = seen(segments[...])
    cos, sin = full_table(cos_full[...], sin_full[...])
    turn = lambda v: (v * cos + pltpu.roll(v, 64, 1) * sin).astype(BF16)
    key = turn(keys[...].astype(F32))
    value = values[...]

    def pair(p, carry):
        for h in (2 * p, 2 * p + 1):
            query = turn(queries[:, lanes(h)].astype(F32))
            weights = softmax(dot_nt(query, key), mask).astype(BF16)
            out[:, lanes(h)] = dot(weights, value)
        return carry

    lax.fori_loop(0, 4, pair, 0)
    half = lambda c: tokens[:, pl.ds(pl.multiple_of(c * 512, 512), 512)].T
    tokens_keep[...] = half(at[0])
    tokens_send[...] = half(1 - at[0]).astype(F32)


def student_kernel(
    at, packed, queries_in, key_up_in, value_up_in, teacher_in, cos_part, sin_part, segments,
    keep_out, send_out, norm_out, latent, rest, nope, head_values, rest_sum, grads,
    queries, key_up, value_up, teacher, keep, send, norm, sems,
):
    (get_keys, get_values, *get_others) = start(
        (key_up_in, key_up, sems.at[0]),
        (value_up_in, value_up, sems.at[1]),
        (queries_in, queries, sems.at[2]),
        (teacher_in, teacher, sems.at[3]),
    )
    unpack(packed, latent, rest)
    cos, sin = part_table(cos_part[...], sin_part[...])
    low = low_lanes(SEQ)
    turn = lambda v: v * cos + swap(v) * sin
    rope_key = turn(rest[...])
    wait([get_keys])
    nope[...] = dot(latent[...], key_up[...])
    wait([get_values])
    head_values[...] = dot(latent[...], value_up[...]).astype(BF16)
    mask = seen(segments[...])
    scale = 1.0 / math.sqrt(HEAD)
    rest_sum[...] = jnp.zeros_like(rest_sum)
    wait(get_others)

    def head(h, key_part):
        query = turn(queries[:, lanes(h)].astype(F32)).astype(BF16)
        key = jnp.where(low, rope_key, key_part).astype(BF16)
        weights = softmax(dot_nt(query, key), mask)
        weights_low = weights.astype(BF16)
        value = head_values[:, lanes(h)]
        out_grad = (dot(weights_low, value) - teacher[:, lanes(h)]).astype(BF16)
        weight_grad = dot_nt(out_grad, value)
        row = jnp.sum(weights * weight_grad, axis=1, keepdims=True)
        score_grad = (weights * (weight_grad - row) * scale).astype(BF16)
        grads[:, lanes(4 + h)] = dot_tn(weights_low, out_grad).astype(BF16)
        return dot_tn(score_grad, query)

    def heads(step, carry):
        for p in (2 * step, 2 * step + 1):
            both = nope[:, lanes(p)]
            first = head(2 * p, pltpu.roll(both, 64, 1))
            second = head(2 * p + 1, both)
            rest_sum[...] += first + second
            grads[:, lanes(p)] = jnp.where(low, pltpu.roll(first, 64, 1), second).astype(BF16)
        return carry

    lax.fori_loop(0, 2, heads, 0)
    for ref, c in ((send, 1 - at[0]), (keep, at[0])):
        keys = pl.ds(pl.multiple_of(c * 256, 256), 256)
        values = pl.ds(pl.multiple_of(512 + c * 512, 512), 512)
        ref[:, :256] = grads[:, keys].astype(ref.dtype)
        ref[:, 256:768] = grads[:, values].astype(ref.dtype)
        ref[:, 768:] = latent[...].astype(ref.dtype)
    puts = start((send, send_out, sems.at[4]), (keep, keep_out, sems.at[5]))
    wide = dot_nt(grads[:, :512], key_up[...]) + dot_nt(grads[:, 512:], value_up[...])
    rest_all = rest_sum[...]
    for k in range(8):
        pack(norm, k, 32 * k, wide, rest_all)
    wait(puts + start((norm, norm_out, sems.at[6])))


def up_kernel(at, own, other, *outs):
    whole = dot_tn(own[:, 768:], own[:, :768])
    whole = whole + dot_tn(other[:, 768:].astype(BF16), other[:, :768].astype(BF16))
    for quarter in range(4):
        for step in range(4):
            @pl.when((at[1] + step) % 4 == quarter)
            def _(quarter=quarter, step=step):
                outs[step][...] = whole[128 * quarter : 128 * quarter + 128]


def halves_kernel(own, first, second, third, *outs):
    n = outs[0].shape[0]
    for k, out in enumerate(outs):
        rows = slice(n * k, n * k + n)
        out[...] = (own[rows] + first[rows]) + (second[rows] + third[rows])


def add_kernel(a, b, got_a, got_b, a_out, b_out):
    a_out[...] = a[...] + got_a[...]
    b_out[...] = b[...] + got_b[...]


def add_stack_kernel(a, b, got_a, got_b, out):
    n = a.shape[0]
    out[:n] = a[...] + got_a[...]
    out[n:] = b[...] + got_b[...]


def entry_grad_kernel(at, packed, other_packed, tokens, other_tokens, *refs):
    *outs, grads, other_grads, rest = refs
    for source, ref in ((packed, grads), (other_packed, other_grads)):
        unpack(source, ref, rest)
        ref[:, 512:] = jnp.where(low_lanes(SEQ), rest[...], 0.0).astype(BF16)
    for step in range(4):
        rows = pl.ds(pl.multiple_of((at[1] + step) % 4 * 128, 128), 128)
        whole = dot(tokens[rows, :], grads[...])
        whole = whole + dot(other_tokens[rows, :].astype(BF16), other_grads[...])
        for k in range(4):
            pack(outs[step], k, 32 * k, whole[:, :512], whole[:, 512:])


def up_out_kernel(at, *refs):
    *parts, key_out, value_out = refs
    for c in range(2):
        column = jnp.where(c == 0, at[0], 1 - at[0])
        keys = pl.ds(pl.multiple_of(column * 256, 256), 256)
        values = pl.ds(pl.multiple_of(column * 512, 512), 512)
        for step in range(4):
            ref = parts[4 * c + step]
            rows = pl.ds(pl.multiple_of((at[1] - step + 4) % 4 * 128, 128), 128)
            key_out[rows, keys] = ref[:, :256]
            value_out[rows, values] = ref[:, 256:]


def entry_out_kernel(own, at, *refs):
    parts, (down_out, rope_out, down, rope, rest, sems) = refs[:4], refs[-6:]
    half = at[0] if own else 1 - at[0]
    copies = []
    for step in range(4):
        first = (at[1] - step + 4) % 4
        for depth in range(4):
            spot = depth * 32
            rows = pl.ds(pl.multiple_of(first * 128 + spot, 32), 32)
            for j in range(4):
                down[rows, 128 * j : 128 * j + 128] = parts[step][depth, 32 * j : 32 * j + 32, :]
            value = parts[step][depth, 128:PACKED, :]
            unpack_rest(value, rest, spot)
        rope[:, lanes(first)] = rest[...].T[:64]
        group = pl.ds(pl.multiple_of(first * 128, 128), 128)
        where = pl.ds(pl.multiple_of(half * 512 + first * 128, 128), 128)
        copies += start(
            (down.at[group, :], down_out.at[where, :], sems.at[step, 0]),
            (rope.at[:, group], rope_out.at[:, where], sems.at[step, 1]),
        )
    wait(copies)


def permute(value, move):
    pairs = []
    for i in range(256):
        d, t = divmod(i, 8)
        at = dict(x=d // 8, h=(d // 2) % 4, c=d % 2, y=t // 2, l=t % 2)
        to = {**at, **move(at)}
        j = (to["x"] * 8 + to["h"] * 2 + to["c"]) * 8 + to["y"] * 2 + to["l"]
        pairs.append((i, j))
    return lax.ppermute(value, AXES, pairs)


def other_core(value):
    return permute(value, lambda at: {"c": 1 - at["c"]})


def around(value, axis):
    values = value if isinstance(value, list) else [value] * 3
    moves = [lambda at, k=k: {axis: (at[axis] + k) % 4} for k in (1, 2, 3)]
    return [permute(v, move) for v, move in zip(values, moves)]


def partners(a, b, masks):
    return [permute(v, lambda at, m=m: {"h": at["h"] ^ m}) for v, m in zip((a, b), masks)]


def exchange(parts):
    return lax.all_to_all(parts, "tensor", 0, 0, tiled=True)


def tables(segments):
    index = jnp.arange(SEQ, dtype=jnp.int32)
    start = jnp.sum((segments[None, :] < segments[:, None]).astype(jnp.int32), axis=1)
    position = (index - start).astype(F32)

    def angles(width):
        exponent = jnp.arange(width // 2, dtype=F32) * (2.0 / width)
        return position[:, None] * jnp.exp(-exponent * jnp.log(F32(THETA)))[None, :]

    full, part = angles(HEAD), angles(ROPE)
    return (jnp.cos(full), jnp.sin(full)), (jnp.cos(part), jnp.sin(part))


def local(tokens, segment_ids, queries, keys, values, down, rope, key_up, value_up):
    tokens, segments, queries = tokens[0], segment_ids[0], queries[0]
    d = lax.axis_index("dp")
    at = jnp.stack([d % 2, d // 8, d // 2 % 4, lax.axis_index("tensor")])
    seg_row = segments[None, :]
    chunks = shape(8, PACKED, 128)
    unpacked = [pltpu.VMEM((SEQ, LATENT), BF16), pltpu.VMEM((SEQ, 128), F32)]

    (part,) = call(entry_kernel, [chunks], tokens, down, rope, flops=2 * 256 * 1024 * 576, mib=60)
    parts = exchange(part)
    full, partial = tables(segments)
    teacher, tokens_keep, tokens_send = call(
        teacher_kernel,
        [shape(SEQ, 1024), shape(512, SEQ, dtype=BF16), shape(512, SEQ)],
        at, queries, keys[0], values[0], *full, seg_row, tokens,
        scalars=1, flops=4 * 8 * 256 * 256 * 128, mib=60,
    )
    tokens_other = other_core(tokens_send)
    parts, teacher = lax.optimization_barrier((parts, teacher))
    replicas, normed, inv = call(norm_kernel, [chunks, shape(128, 128), shape(32, 128)], parts)
    packed = exchange(replicas)
    grads_keep, grads_send, part = call(
        student_kernel,
        [shape(SEQ, 1280, dtype=BF16), shape(SEQ, 1280), chunks],
        at, packed, queries, key_up, value_up, teacher, *partial, seg_row,
        scalars=1,
        scratch=unpacked + [
            pltpu.VMEM((SEQ, 512), F32),
            pltpu.VMEM((SEQ, 1024), BF16),
            pltpu.VMEM((SEQ, 128), F32),
            pltpu.VMEM((SEQ, 1536), BF16),
            pltpu.VMEM((SEQ, 1024), BF16),
            pltpu.VMEM((LATENT, 512), BF16),
            pltpu.VMEM((LATENT, 1024), BF16),
            pltpu.VMEM((SEQ, 1024), F32),
            pltpu.VMEM((SEQ, 1280), BF16),
            pltpu.VMEM((SEQ, 1280), F32),
            pltpu.VMEM((8, PACKED, 128), F32),
            pltpu.SemaphoreType.DMA((7,)),
        ],
        hbm=(2, 3, 4, 5), hbm_out=True,
        flops=10 * 8 * 256 * 256 * 128, mib=60,
    )
    grads_other = other_core(grads_send)
    parts = exchange(part)
    quarters = call(
        up_kernel, [shape(128, 768)] * 4, at, grads_keep, grads_other,
        scalars=1, flops=2 * 512 * 512 * 768, mib=60,
    )
    received = around(list(quarters[1:]), "x")
    (replicas,) = call(norm_grad_kernel, [chunks], at, parts, normed, inv, *partial, scalars=1)
    packed = exchange(replicas)
    packed_other = other_core(packed)
    halves = call(halves_kernel, [shape(64, 768)] * 2, quarters[0], *received)
    received = partners(*halves, (1, 3))
    entries = call(
        entry_grad_kernel, [shape(4, PACKED, 128)] * 4,
        at, packed, packed_other, tokens_keep, tokens_other, scalars=1,
        scratch=[pltpu.VMEM((SEQ, 640), BF16)] * 2 + [pltpu.VMEM((SEQ, 128), F32)],
        flops=2 * 512 * 512 * 640,
    )
    arrived = around(list(entries[1:]), "x")
    halves = call(add_kernel, [shape(64, 768)] * 2, *halves, *received)
    received = partners(*halves, (3, 1))
    entry = call(halves_kernel, [shape(2, PACKED, 128)] * 2, entries[0], *arrived)
    arrived = partners(*entry, (1, 3))
    (up,) = call(add_stack_kernel, [shape(128, 768)], *halves, *received)
    received = [up] + around(up, "x")
    entry = call(add_kernel, [shape(2, PACKED, 128)] * 2, *entry, *arrived)
    arrived = partners(*entry, (3, 1))
    (entry,) = call(add_stack_kernel, [shape(4, PACKED, 128)], *entry, *arrived)
    entries = [entry] + around(entry, "x")
    others = [other_core(v) for v in received]
    grad_key, grad_value = call(
        up_out_kernel, [shape(512, 512), shape(512, 1024)], at, *received, *others, scalars=1,
    )
    others = [other_core(v) for v in entries]
    outs = [shape(1024, 512), shape(64, 1024)]
    scratch = [
        pltpu.VMEM((512, 512), F32),
        pltpu.VMEM((64, 512), F32),
        pltpu.VMEM((128, 128), F32),
        pltpu.SemaphoreType.DMA((4, 2)),
    ]
    halves = call(
        functools.partial(entry_out_kernel, True), outs, at, *entries, scalars=1,
        scratch=scratch, hbm_out=True,
    )
    grad_down, grad_rope = call(
        functools.partial(entry_out_kernel, False), outs, at, *others, *halves, scalars=1,
        scratch=scratch, hbm_out=True, aliases={5: 0, 6: 1},
    )
    return grad_down, grad_rope, grad_key, grad_value


def solution(mesh):
    token = P("dp", None, "tensor")
    rows, columns = P("tensor", None), P(None, "tensor")
    in_specs = (token, P("dp", None), token, token, token, rows, columns, columns, columns)
    out_specs = (rows, columns, columns, columns)
    return jax.shard_map(local, mesh=mesh, in_specs=in_specs, out_specs=out_specs, check_vma=False)
```

```python
import functools
import math

import jax
import jax.numpy as jnp
from jax import lax
from jax.experimental import pallas as pl
from jax.experimental.pallas import tpu as pltpu
from jax.sharding import PartitionSpec as P


HEAD = 128
ROPE = 64
SEQ = 256
LATENT = 512
THETA = 500000.0
EPS = 1e-06
AXES = ("dp", "tensor")
F32 = jnp.float32
BF16 = jnp.bfloat16

NT = (((1,), (1,)), ((), ()))
TN = (((0,), (0,)), ((), ()))
PACKED = 144


def dot(a, b):
    return jnp.dot(a, b, preferred_element_type=F32)


def dot_nt(a, b):
    return lax.dot_general(a, b, NT, preferred_element_type=F32)


def dot_tn(a, b):
    return lax.dot_general(a, b, TN, preferred_element_type=F32)


def call(body, outs, *args, scalars=0, scratch=(), flops=0, mib=20,
         aliases=None, hbm=(), hbm_out=False):
    spec = pl.BlockSpec(memory_space=pltpu.VMEM)
    smem = pl.BlockSpec(memory_space=pltpu.SMEM)
    anywhere = pl.BlockSpec(memory_space=pltpu.HBM)
    specs = [smem] * scalars + [spec] * (len(args) - scalars)
    for k in (*(aliases or {}), *hbm):
        specs[k] = anywhere
    size = sum(a.size * a.dtype.itemsize for a in args)
    size += sum(math.prod(o.shape) * o.dtype.itemsize for o in outs)
    return pl.pallas_call(
        body,
        out_shape=outs,
        in_specs=specs,
        out_specs=[anywhere if hbm_out else spec] * len(outs),
        scratch_shapes=list(scratch),
        input_output_aliases=aliases or {},
        compiler_params=pltpu.CompilerParams(vmem_limit_bytes=mib << 20),
        cost_estimate=pl.CostEstimate(flops=flops, bytes_accessed=size, transcendentals=0),
    )(*args)


def shape(*dims, dtype=F32):
    return jax.ShapeDtypeStruct(dims, dtype)


def low_lanes(rows):
    return lax.broadcasted_iota(jnp.int32, (rows, 128), 1) < 64


def pack_rest(first, second):
    return jnp.where(low_lanes(16), first, pltpu.roll(second, 64, 1))


def swap(value):
    lane = lax.broadcasted_iota(jnp.int32, value.shape, 1)
    return jnp.where(lane < 32, pltpu.roll(value, 96, 1), pltpu.roll(value, 32, 1))


def pack(out, k, rows, wide, rest):
    for j in range(4):
        out[k, 32 * j : 32 * j + 32, :] = wide[rows : rows + 32, 128 * j : 128 * j + 128]
    out[k, 128:PACKED, :] = pack_rest(rest[rows : rows + 16], rest[rows + 16 : rows + 32])


def unpack_rest(value, out, rows):
    out[rows : rows + 16, :] = value
    out[rows + 16 : rows + 32, :] = pltpu.roll(value, 64, 1)


def unpack(packed, wide, rest):
    for k in range(8):
        for j in range(4):
            wide[32 * k : 32 * k + 32, 128 * j : 128 * j + 128] = packed[
                k, 32 * j : 32 * j + 32, :
            ].astype(wide.dtype)
        unpack_rest(packed[k, 128:PACKED, :], rest, 32 * k)


def start(*pairs):
    copies = [pltpu.make_async_copy(source, target, sem) for source, target, sem in pairs]
    for copy in copies:
        copy.start()
    return copies


def wait(copies):
    for copy in copies:
        copy.wait()


def entry_kernel(tokens, down, rope, out):
    wide = dot(tokens[...], down[...])
    rest = dot_nt(tokens[...], rope[...])
    rest = jnp.concatenate([rest, jnp.zeros_like(rest)], axis=1)
    for k in range(8):
        pack(out, k, 32 * k, wide, rest)


def norm_kernel(parts, out, normed_out, inv_out):
    total = jnp.sum(parts[...], axis=0)
    square = jnp.zeros((32, 1), F32)
    for j in range(4):
        tile = total[32 * j : 32 * j + 32]
        square = square + jnp.sum(tile * tile, axis=1, keepdims=True)
    inv = lax.rsqrt(square * (1.0 / LATENT) + EPS)
    inv = jnp.broadcast_to(inv, (32, 128))
    inv_out[...] = inv
    normed = total[:128] * jnp.concatenate([inv] * 4, axis=0)
    normed_out[...] = normed
    for k in range(8):
        out[k, :128, :] = normed
        out[k, 128:, :] = total[128:]


def norm_grad_kernel(at, parts, normed, inv, cos_part, sin_part, out):
    total = jnp.sum(parts[...], axis=0)
    rows = pl.ds(pl.multiple_of(at[3] * 32, 32), 32)
    rest = jnp.concatenate([total[128:], pltpu.roll(total[128:], 64, 1)], axis=0)
    cos, sin = part_table(cos_part[rows, :], sin_part[rows, :])
    rest = rest * cos - swap(rest) * sin
    rest = pack_rest(rest[:16], rest[16:])
    grad = total[:128]
    product = grad * normed[...]
    mean = jnp.zeros((32, 1), F32)
    for j in range(4):
        mean = mean + jnp.sum(product[32 * j : 32 * j + 32], axis=1, keepdims=True)
    mean = jnp.broadcast_to(mean * (1.0 / LATENT), (32, 128))
    four = lambda v: jnp.concatenate([v] * 4, axis=0)
    grad = (grad - normed[...] * four(mean)) * four(inv[...])
    for k in range(8):
        out[k, :128, :] = grad
        out[k, 128:, :] = rest


def full_table(cos, sin):
    return jnp.concatenate([cos, cos], axis=1), jnp.concatenate([-sin, sin], axis=1)


def part_table(cos, sin):
    one, zero = jnp.ones((cos.shape[0], 64), F32), jnp.zeros((cos.shape[0], 64), F32)
    return jnp.concatenate([cos, cos, one], axis=1), jnp.concatenate([-sin, sin, zero], axis=1)


def seen(seg_row):
    seg_col = jnp.broadcast_to(seg_row, (8, SEQ)).T[:, :1]
    i = lax.broadcasted_iota(jnp.int32, (SEQ, SEQ), 0)
    j = lax.broadcasted_iota(jnp.int32, (SEQ, SEQ), 1)
    return (seg_col == seg_row) & (j <= i)


def softmax(scores, mask):
    scores = jnp.where(mask, scores * (1.0 / math.sqrt(HEAD)), -3e38)
    weights = jnp.exp(scores - jnp.max(scores, axis=1, keepdims=True))
    return weights * (1.0 / jnp.sum(weights, axis=1, keepdims=True))


def lanes(h):
    return pl.ds(pl.multiple_of(h * 128, 128), 128)


def teacher_kernel(
    at, queries, keys, values, cos_full, sin_full, segments, tokens, out, tokens_keep, tokens_send
):
    mask = seen(segments[...])
    cos, sin = full_table(cos_full[...], sin_full[...])
    turn = lambda v: (v * cos + pltpu.roll(v, 64, 1) * sin).astype(BF16)
    key = turn(keys[...].astype(F32))
    value = values[...]

    def pair(p, carry):
        for h in (2 * p, 2 * p + 1):
            query = turn(queries[:, lanes(h)].astype(F32))
            weights = softmax(dot_nt(query, key), mask).astype(BF16)
            out[:, lanes(h)] = dot(weights, value)
        return carry

    lax.fori_loop(0, 4, pair, 0)
    half = lambda c: tokens[:, pl.ds(pl.multiple_of(c * 512, 512), 512)].T
    tokens_keep[...] = half(at[0])
    tokens_send[...] = half(1 - at[0]).astype(F32)


def student_kernel(
    at, packed, queries_in, key_up_in, value_up_in, teacher_in, cos_part, sin_part, segments,
    keep_out, send_out, norm_out, latent, rest, nope, head_values, rest_sum, grads,
    queries, key_up, value_up, teacher, keep, send, norm, sems,
):
    (get_keys, get_values, *get_others) = start(
        (key_up_in, key_up, sems.at[0]),
        (value_up_in, value_up, sems.at[1]),
        (queries_in, queries, sems.at[2]),
        (teacher_in, teacher, sems.at[3]),
    )
    unpack(packed, latent, rest)
    cos, sin = part_table(cos_part[...], sin_part[...])
    low = low_lanes(SEQ)
    turn = lambda v: v * cos + swap(v) * sin
    rope_key = turn(rest[...])
    wait([get_keys])
    nope[...] = dot(latent[...], key_up[...])
    wait([get_values])
    head_values[...] = dot(latent[...], value_up[...]).astype(BF16)
    mask = seen(segments[...])
    scale = 1.0 / math.sqrt(HEAD)
    rest_sum[...] = jnp.zeros_like(rest_sum)
    wait(get_others)

    def head(h, key_part):
        query = turn(queries[:, lanes(h)].astype(F32)).astype(BF16)
        key = jnp.where(low, rope_key, key_part).astype(BF16)
        weights = softmax(dot_nt(query, key), mask)
        weights_low = weights.astype(BF16)
        value = head_values[:, lanes(h)]
        out_grad = (dot(weights_low, value) - teacher[:, lanes(h)]).astype(BF16)
        weight_grad = dot_nt(out_grad, value)
        row = jnp.sum(weights * weight_grad, axis=1, keepdims=True)
        score_grad = (weights * (weight_grad - row) * scale).astype(BF16)
        grads[:, lanes(4 + h)] = dot_tn(weights_low, out_grad).astype(BF16)
        return dot_tn(score_grad, query)

    def heads(step, carry):
        for p in (4 * step, 4 * step + 1, 4 * step + 2, 4 * step + 3):
            both = nope[:, lanes(p)]
            first = head(2 * p, pltpu.roll(both, 64, 1))
            second = head(2 * p + 1, both)
            rest_sum[...] += first + second
            grads[:, lanes(p)] = jnp.where(low, pltpu.roll(first, 64, 1), second).astype(BF16)
        return carry

    lax.fori_loop(0, 1, heads, 0)
    for ref, c in ((send, 1 - at[0]), (keep, at[0])):
        keys = pl.ds(pl.multiple_of(c * 256, 256), 256)
        values = pl.ds(pl.multiple_of(512 + c * 512, 512), 512)
        ref[:, :256] = grads[:, keys].astype(ref.dtype)
        ref[:, 256:] = grads[:, values].astype(ref.dtype)
    puts = start((send, send_out, sems.at[4]), (keep, keep_out, sems.at[5]))
    wide = dot_nt(grads[:, :512], key_up[...]) + dot_nt(grads[:, 512:], value_up[...])
    rest_all = rest_sum[...]
    for k in range(8):
        pack(norm, k, 32 * k, wide, rest_all)
    wait(puts + start((norm, norm_out, sems.at[6])))


def up_kernel(at, packed, other_packed, grads, other_grads, *outs):
    *outs, latent, rest = outs
    unpack(packed, latent, rest)
    whole = dot_tn(latent[...], grads[...])
    unpack(other_packed, latent, rest)
    whole = whole + dot_tn(latent[...], other_grads[...].astype(BF16))
    for quarter in range(4):
        for step in range(4):
            @pl.when((at[1] + step) % 4 == quarter)
            def _(quarter=quarter, step=step):
                outs[step][...] = whole[128 * quarter : 128 * quarter + 128]


def halves_kernel(own, first, second, third, *outs):
    n = outs[0].shape[0]
    for k, out in enumerate(outs):
        rows = slice(n * k, n * k + n)
        out[...] = (own[rows] + first[rows]) + (second[rows] + third[rows])


def add_kernel(a, b, got_a, got_b, a_out, b_out):
    a_out[...] = a[...] + got_a[...]
    b_out[...] = b[...] + got_b[...]


def add_stack_kernel(a, b, got_a, got_b, out):
    n = a.shape[0]
    out[:n] = a[...] + got_a[...]
    out[n:] = b[...] + got_b[...]


def entry_grad_kernel(at, packed, other_packed, tokens, other_tokens, *refs):
    *outs, grads, other_grads, rest = refs
    for source, ref in ((packed, grads), (other_packed, other_grads)):
        unpack(source, ref, rest)
        ref[:, 512:] = jnp.where(low_lanes(SEQ), rest[...], 0.0).astype(BF16)
    for step in range(4):
        rows = pl.ds(pl.multiple_of((at[1] + step) % 4 * 128, 128), 128)
        whole = dot(tokens[rows, :], grads[...])
        whole = whole + dot(other_tokens[rows, :].astype(BF16), other_grads[...])
        for k in range(4):
            pack(outs[step], k, 32 * k, whole[:, :512], whole[:, 512:])


def up_out_kernel(at, *refs):
    *parts, key_out, value_out = refs
    for c in range(2):
        column = jnp.where(c == 0, at[0], 1 - at[0])
        keys = pl.ds(pl.multiple_of(column * 256, 256), 256)
        values = pl.ds(pl.multiple_of(column * 512, 512), 512)
        for step in range(4):
            ref = parts[4 * c + step]
            rows = pl.ds(pl.multiple_of((at[1] - step + 4) % 4 * 128, 128), 128)
            key_out[rows, keys] = ref[:, :256]
            value_out[rows, values] = ref[:, 256:]


def entry_out_kernel(own, at, *refs):
    parts, (down_out, rope_out, down, rope, rest, sems) = refs[:4], refs[-6:]
    half = at[0] if own else 1 - at[0]
    copies = []
    for step in range(4):
        first = (at[1] - step + 4) % 4
        for depth in range(4):
            spot = depth * 32
            rows = pl.ds(pl.multiple_of(first * 128 + spot, 32), 32)
            for j in range(4):
                down[rows, 128 * j : 128 * j + 128] = parts[step][depth, 32 * j : 32 * j + 32, :]
            value = parts[step][depth, 128:PACKED, :]
            unpack_rest(value, rest, spot)
        rope[:, lanes(first)] = rest[...].T[:64]
        group = pl.ds(pl.multiple_of(first * 128, 128), 128)
        where = pl.ds(pl.multiple_of(half * 512 + first * 128, 128), 128)
        copies += start(
            (down.at[group, :], down_out.at[where, :], sems.at[step, 0]),
            (rope.at[:, group], rope_out.at[:, where], sems.at[step, 1]),
        )
    wait(copies)


def permute(value, move):
    pairs = []
    for i in range(256):
        d, t = divmod(i, 8)
        at = dict(x=d // 8, h=(d // 2) % 4, c=d % 2, y=t // 2, l=t % 2)
        to = {**at, **move(at)}
        j = (to["x"] * 8 + to["h"] * 2 + to["c"]) * 8 + to["y"] * 2 + to["l"]
        pairs.append((i, j))
    return lax.ppermute(value, AXES, pairs)


def other_core(value):
    return permute(value, lambda at: {"c": 1 - at["c"]})


def around(value, axis):
    values = value if isinstance(value, list) else [value] * 3
    moves = [lambda at, k=k: {axis: (at[axis] + k) % 4} for k in (1, 2, 3)]
    return [permute(v, move) for v, move in zip(values, moves)]


def partners(a, b, masks):
    return [permute(v, lambda at, m=m: {"h": at["h"] ^ m}) for v, m in zip((a, b), masks)]


def exchange(parts):
    return lax.all_to_all(parts, "tensor", 0, 0, tiled=True)


def tables(segments):
    index = jnp.arange(SEQ, dtype=jnp.int32)
    start = jnp.sum((segments[None, :] < segments[:, None]).astype(jnp.int32), axis=1)
    position = (index - start).astype(F32)

    def angles(width):
        exponent = jnp.arange(width // 2, dtype=F32) * (2.0 / width)
        return position[:, None] * jnp.exp(-exponent * jnp.log(F32(THETA)))[None, :]

    full, part = angles(HEAD), angles(ROPE)
    return (jnp.cos(full), jnp.sin(full)), (jnp.cos(part), jnp.sin(part))


def local(tokens, segment_ids, queries, keys, values, down, rope, key_up, value_up):
    tokens, segments, queries = tokens[0], segment_ids[0], queries[0]
    d = lax.axis_index("dp")
    at = jnp.stack([d % 2, d // 8, d // 2 % 4, lax.axis_index("tensor")])
    seg_row = segments[None, :]
    chunks = shape(8, PACKED, 128)
    unpacked = [pltpu.VMEM((SEQ, LATENT), BF16), pltpu.VMEM((SEQ, 128), F32)]

    (part,) = call(entry_kernel, [chunks], tokens, down, rope, flops=2 * 256 * 1024 * 576, mib=60)
    parts = exchange(part)
    full, partial = tables(segments)
    teacher, tokens_keep, tokens_send = call(
        teacher_kernel,
        [shape(SEQ, 1024), shape(512, SEQ, dtype=BF16), shape(512, SEQ)],
        at, queries, keys[0], values[0], *full, seg_row, tokens,
        scalars=1, flops=4 * 8 * 256 * 256 * 128, mib=60,
    )
    tokens_other = other_core(tokens_send)
    parts, teacher = lax.optimization_barrier((parts, teacher))
    replicas, normed, inv = call(norm_kernel, [chunks, shape(128, 128), shape(32, 128)], parts)
    packed = exchange(replicas)
    packed_other = other_core(packed)
    grads_keep, grads_send, part = call(
        student_kernel,
        [shape(SEQ, 768, dtype=BF16), shape(SEQ, 768), chunks],
        at, packed, queries, key_up, value_up, teacher, *partial, seg_row,
        scalars=1,
        scratch=unpacked + [
            pltpu.VMEM((SEQ, 512), F32),
            pltpu.VMEM((SEQ, 1024), BF16),
            pltpu.VMEM((SEQ, 128), F32),
            pltpu.VMEM((SEQ, 1536), BF16),
            pltpu.VMEM((SEQ, 1024), BF16),
            pltpu.VMEM((LATENT, 512), BF16),
            pltpu.VMEM((LATENT, 1024), BF16),
            pltpu.VMEM((SEQ, 1024), F32),
            pltpu.VMEM((SEQ, 768), BF16),
            pltpu.VMEM((SEQ, 768), F32),
            pltpu.VMEM((8, PACKED, 128), F32),
            pltpu.SemaphoreType.DMA((7,)),
        ],
        hbm=(2, 3, 4, 5), hbm_out=True,
        flops=10 * 8 * 256 * 256 * 128, mib=60,
    )
    grads_other = other_core(grads_send)
    parts = exchange(part)
    quarters = call(
        up_kernel, [shape(128, 768)] * 4, at, packed, packed_other, grads_keep, grads_other,
        scalars=1, scratch=unpacked, flops=2 * 512 * 512 * 768, mib=60,
    )
    received = around(list(quarters[1:]), "x")
    (replicas,) = call(norm_grad_kernel, [chunks], at, parts, normed, inv, *partial, scalars=1)
    packed = exchange(replicas)
    packed_other = other_core(packed)
    halves = call(halves_kernel, [shape(64, 768)] * 2, quarters[0], *received)
    received = partners(*halves, (1, 3))
    entries = call(
        entry_grad_kernel, [shape(4, PACKED, 128)] * 4,
        at, packed, packed_other, tokens_keep, tokens_other, scalars=1,
        scratch=[pltpu.VMEM((SEQ, 640), BF16)] * 2 + [pltpu.VMEM((SEQ, 128), F32)],
        flops=2 * 512 * 512 * 640,
    )
    arrived = around(list(entries[1:]), "x")
    halves = call(add_kernel, [shape(64, 768)] * 2, *halves, *received)
    received = partners(*halves, (3, 1))
    entry = call(halves_kernel, [shape(2, PACKED, 128)] * 2, entries[0], *arrived)
    arrived = partners(*entry, (1, 3))
    (up,) = call(add_stack_kernel, [shape(128, 768)], *halves, *received)
    received = [up] + around(up, "x")
    entry = call(add_kernel, [shape(2, PACKED, 128)] * 2, *entry, *arrived)
    arrived = partners(*entry, (3, 1))
    (entry,) = call(add_stack_kernel, [shape(4, PACKED, 128)], *entry, *arrived)
    entries = [entry] + around(entry, "x")
    others = [other_core(v) for v in received]
    grad_key, grad_value = call(
        up_out_kernel, [shape(512, 512), shape(512, 1024)], at, *received, *others, scalars=1,
    )
    others = [other_core(v) for v in entries]
    outs = [shape(1024, 512), shape(64, 1024)]
    scratch = [
        pltpu.VMEM((512, 512), F32),
        pltpu.VMEM((64, 512), F32),
        pltpu.VMEM((128, 128), F32),
        pltpu.SemaphoreType.DMA((4, 2)),
    ]
    halves = call(
        functools.partial(entry_out_kernel, True), outs, at, *entries, scalars=1,
        scratch=scratch, hbm_out=True,
    )
    grad_down, grad_rope = call(
        functools.partial(entry_out_kernel, False), outs, at, *others, *halves, scalars=1,
        scratch=scratch, hbm_out=True, aliases={5: 0, 6: 1},
    )
    return grad_down, grad_rope, grad_key, grad_value


def solution(mesh):
    token = P("dp", None, "tensor")
    rows, columns = P("tensor", None), P(None, "tensor")
    in_specs = (token, P("dp", None), token, token, token, rows, columns, columns, columns)
    out_specs = (rows, columns, columns, columns)
    return jax.shard_map(local, mesh=mesh, in_specs=in_specs, out_specs=out_specs, check_vma=False)
```
